256 devices in a mesh: energy: 64 (over y_lo, z, x), tile: 4 (over y_hi, core).
Axes of the slice: x: 4, y: 4 (y_hi: 2, y_lo: 2; y = y_hi * 2 + y_lo), z: 8, core: 2. Of those that a mesh axis runs over, the one named last changes fastest.
Arguments:
- material_maps: float32 [2, 4, 256, 1024], P(None, None, 'energy', 'tile'), may hold values from -0.3 to 0.3
- spectra: float32 [64, 4, 2], replicated, may hold values from -0.3 to 0.3
- probes: float32 [64, 128, 256], P('energy'), may hold values from -1 to 1, as said below
- offsets: int32 [4, 32, 2], P('tile'), may hold values from 0 to 128
- measured: float32 [64, 4, 32, 128, 128], P('energy', 'tile'), may hold values from 0 to 4
Outputs:
- refined_maps: float32 [2, 4, 256, 1024], P(None, None, 'energy', 'tile')
The draws below stay inside these ranges and needn't reach their ends.
Inputs may be any that keep to these rules, and one draw needn't show every extreme that they name: `probes`: each probe entry has modulus between 0.5 and 1.
All inputs are finite; a program needn't handle non-finite values.
Results may differ from the reference program's by a relative error of at most 0.0024.
The reference program's roundings to bfloat16 on the way count: a program that leaves them out, or rounds other values in their place, can miss the bound.
Values sent between devices are 32-bit elements; how exact they have to be, the bound alone decides.
No kernel may reach another device: no remote copies, remote signals or barrier semaphores. Data moves between devices by JAX's collectives and lax.ppermute only.
A program may use at most 64 MiB of HBM per device.

```python
import math
import jax
import jax.numpy as jnp
from jax import lax

MAT = 4
PATCH = 128
TILE = 256
PATCHES = 32
ITERS = 2
TV_STEPS = 3
ENERGIES = 64
TILES = 4


def draw_probes(key, part):
    amp_key = jax.random.fold_in(key, 11)
    angle_key = jax.random.fold_in(key, 12)
    amplitude = jax.random.uniform(amp_key, (ENERGIES, PATCH, PATCH), jnp.float32, 0.5, 1.0)
    angle = jax.random.uniform(angle_key, (ENERGIES, PATCH, PATCH), jnp.float32, -math.pi, math.pi)
    return jnp.concatenate([amplitude * jnp.cos(angle), amplitude * jnp.sin(angle)], axis=-1).astype(jnp.float32)


def with_ends(values, key, low, largest):
    spot = [jax.random.randint(jax.random.fold_in(key, axis), (), 0, length) for axis, length in enumerate(values.shape)]
    widest = values.shape.index(max(values.shape))
    neighbour = spot[:widest] + [(spot[widest] + 1) % values.shape[widest]] + spot[widest + 1:]
    return values.at[tuple(spot)].set(low).at[tuple(neighbour)].set(largest)


def block_scale(key, dims, shards, smallest, largest):
    def one(position, parts):
        steps = jax.random.uniform(jax.random.fold_in(jax.random.fold_in(key, 6), position), (parts,), jnp.float32, smallest / len(shards), largest / len(shards))
        return jnp.repeat(jnp.exp(steps), dims[position] // parts).reshape((-1,) + (1,) * (len(dims) - position - 1))

    factor_of = one(*shards[0])
    for cut in shards[1:]:
        factor_of = factor_of * one(*cut)
    return factor_of


def setup_inputs(seed: int = 0) -> dict:
    key_list = jax.random.split(jax.random.key(seed), 6)
    material_maps = jnp.clip(jax.random.uniform(key_list[0], (2, MAT, TILE, TILE * TILES), jnp.float32, -0.3, 0.3) * block_scale(key_list[0], (2, MAT, TILE, TILE * TILES), ((2, 64), (3, 4)), -0.4, 0.0), -0.3, 0.3)
    spectra = jnp.clip(jax.random.uniform(key_list[1], (ENERGIES, MAT, 2), jnp.float32, -0.3, 0.3), -0.3, 0.3)
    probes = draw_probes(jax.random.fold_in(key_list[5], 71), 0)
    offsets = with_ends(jax.random.randint(key_list[3], (TILES, PATCHES, 2), 0, TILE - PATCH + 1), jax.random.fold_in(key_list[3], 1), 0, TILE - PATCH).astype(jnp.int32)
    measured = jnp.clip(4.0 * jax.random.uniform(key_list[4], (ENERGIES, TILES, PATCHES, PATCH, PATCH), jnp.float32) ** block_scale(key_list[4], (ENERGIES, TILES, PATCHES, PATCH, PATCH), ((0, 64), (1, 4)), -0.2, 0.2), 0.0, 4.0)
    return {"material_maps": material_maps, "spectra": spectra, "probes": probes, "offsets": offsets, "measured": measured}


DATA_STEP = 0.05
TV_STEP = 0.05
TV_EPS = 0.01

def dft_tables(length):
    index = jnp.arange(length, dtype=jnp.int32)
    phase = index[:, None] * index[None, :] % length
    angle = phase.astype(jnp.float32) * (-2.0 * math.pi / length)
    scale = 1.0 / math.sqrt(length)
    return ((jnp.cos(angle) * scale).astype(jnp.bfloat16), (jnp.sin(angle) * scale).astype(jnp.bfloat16))

def dft_blocks(real_table, imag_table):
    right_fwd = jnp.concatenate([jnp.concatenate([real_table, imag_table], 1), jnp.concatenate([-imag_table, real_table], 1)], 0)
    right_back = jnp.concatenate([jnp.concatenate([real_table, -imag_table], 1), jnp.concatenate([imag_table, real_table], 1)], 0)
    stacked = jnp.concatenate([real_table, imag_table], 0)
    return (right_fwd, right_back, stacked)

def mix(columns, weights):
    real_part = jnp.zeros(columns.shape[2:], jnp.float32)
    imag_part = jnp.zeros(columns.shape[2:], jnp.float32)
    for material in range(columns.shape[1]):
        real_part = real_part + weights[material, 0] * columns[0, material] - weights[material, 1] * columns[1, material]
        imag_part = imag_part + weights[material, 0] * columns[1, material] + weights[material, 1] * columns[0, material]
    return (real_part, imag_part)

def exponent(real_part, imag_part):
    growth = jnp.exp(real_part)
    return jnp.stack([growth * jnp.cos(imag_part), growth * jnp.sin(imag_part)], axis=1)

def conj_times(wave, other):
    return jnp.stack([wave[:, 0] * other[:, 0] + wave[:, 1] * other[:, 1], wave[:, 0] * other[:, 1] - wave[:, 1] * other[:, 0]], axis=1)

def spectral(grad_exp, weights):
    grad_real = grad_exp[:, 0]
    grad_imag = grad_exp[:, 1]
    reals = [weights[material, 0] * grad_real + weights[material, 1] * grad_imag for material in range(weights.shape[0])]
    imags = [weights[material, 0] * grad_imag - weights[material, 1] * grad_real for material in range(weights.shape[0])]
    return jnp.stack([jnp.stack(reals, 0), jnp.stack(imags, 0)], 0)

def tv_div(extended):
    base = extended[:, :, :-1, :-1]
    down = extended[:, :, 1:, :-1] - base
    across = extended[:, :, :-1, 1:] - base
    magnitude = jnp.sqrt(lax.optimization_barrier(jnp.sum(down * down + across * across, axis=0)) + TV_EPS)
    norm_down = down / magnitude
    norm_across = across / magnitude
    return norm_down[:, :, 1:, 1:] - norm_down[:, :, :-1, 1:] + norm_across[:, :, 1:, 1:] - norm_across[:, :, 1:, :-1]

def product(left, right):
    return jnp.dot(left.astype(jnp.float32), right.astype(jnp.float32), precision=lax.Precision.HIGHEST)

def patch_gradient(piece, my_probe, counts, blocks):
    right_fwd, right_back, stacked = blocks
    length = my_probe.shape[0]
    probe_real = my_probe[:, :length]
    probe_imag = my_probe[:, length:]
    wave_real = piece[:, 0]
    wave_imag = piece[:, 1]
    exit_wave = jnp.concatenate([probe_real * wave_real - probe_imag * wave_imag, probe_real * wave_imag + probe_imag * wave_real], axis=-1).astype(jnp.bfloat16)
    first_pass = product(exit_wave, right_fwd).astype(jnp.bfloat16)
    second_pass = product(stacked, first_pass)
    far_real = second_pass[:length, :length] - second_pass[length:, length:]
    far_imag = second_pass[:length, length:] + second_pass[length:, :length]
    misfit = far_real * far_real + far_imag * far_imag - counts
    weighted = jnp.concatenate([misfit * far_real, misfit * far_imag], axis=-1).astype(jnp.bfloat16)
    third_pass = product(weighted, right_back).astype(jnp.bfloat16)
    fourth_pass = product(stacked, third_pass)
    grad_real = fourth_pass[:length, :length] + fourth_pass[length:, length:]
    grad_imag = fourth_pass[:length, length:] - fourth_pass[length:, :length]
    return jnp.stack([probe_real * grad_real + probe_imag * grad_imag, probe_real * grad_imag - probe_imag * grad_real], axis=1)

def tile_gradient(tile_wave, my_probe, my_spots, my_data, blocks):

    def cut(location):
        return lax.dynamic_slice(tile_wave, (location[0], location[0] * 0, location[1]), (PATCH, 2, PATCH))
    pieces = jax.vmap(cut)(my_spots)
    updates = jax.vmap(lambda piece_one, count_one: patch_gradient(piece_one, my_probe, count_one, blocks))(pieces, my_data)

    def place(running, item):
        location, update = item
        corner = (location[0], location[0] * 0, location[1])
        before = lax.dynamic_slice(running, corner, (PATCH, 2, PATCH))
        return (lax.dynamic_update_slice(running, before + update, corner), None)
    result, _ = lax.scan(place, jnp.zeros(tile_wave.shape, jnp.float32), (my_spots, updates))
    return result

def reference(material_maps, spectra, probes, offsets, measured):
    blocks = dft_blocks(*dft_tables(PATCH))
    factor = DATA_STEP / math.sqrt(ENERGIES)
    current = material_maps
    for repeat in range(ITERS):

        def per_energy(running, inputs):
            weights, my_probe, my_data = inputs
            terms = []
            for tile_index in range(TILES):
                columns = current[:, :, :, tile_index * TILE:(tile_index + 1) * TILE]
                tile_wave = exponent(*mix(columns, weights))
                grad_wave = tile_gradient(tile_wave, my_probe, offsets[tile_index], my_data[tile_index], blocks)
                terms.append(spectral(conj_times(tile_wave, grad_wave), weights))
            return (running + jnp.concatenate(terms, axis=3), None)
        total_grad, _ = lax.scan(per_energy, jnp.zeros(current.shape, jnp.float32), (spectra, probes, measured))
        current = current - factor * total_grad
        for smooth_pass in range(TV_STEPS):
            current = current + TV_STEP * tv_div(jnp.pad(current, ((0, 0), (0, 0), (1, 1), (1, 1))))
    return current
```

```python
import functools
import math

import jax
import jax.numpy as jnp
from jax import lax
from jax.experimental import pallas as pl
from jax.experimental.pallas import tpu as pltpu
from jax.sharding import PartitionSpec as P

ITERS = 2
TV_STEPS = 3
DATA_STEP = 0.05
TV_STEP = 0.05
TV_EPS = 0.01

LEN = 128
GROUP = 8

def dft_tables(length):
    index = jnp.arange(length, dtype=jnp.int32)
    phase = index[:, None] * index[None, :] % length
    angle = phase.astype(jnp.float32) * (-2.0 * math.pi / length)
    scale = 1.0 / math.sqrt(length)
    return (
        (jnp.cos(angle) * scale).astype(jnp.bfloat16),
        (jnp.sin(angle) * scale).astype(jnp.bfloat16),
    )

def dft_blocks(fr, fi):
    ahead = jnp.concatenate([jnp.concatenate([fr, fi], 1), jnp.concatenate([-fi, fr], 1)], 0)
    back = jnp.concatenate([jnp.concatenate([fr, -fi], 1), jnp.concatenate([fi, fr], 1)], 0)
    return ahead, back

def dot(left, right):
    return jnp.dot(left, right, preferred_element_type=jnp.float32)

def pair_up(both):
    one, two = both
    return jnp.concatenate([
        jnp.concatenate([one[:, :LEN], two[:, :LEN]], 1),
        jnp.concatenate([one[:, LEN:], two[:, LEN:]], 1)], 0)

def patch_kernel(group, spots, z_ref, probe_ref, counts_hbm, ahead_ref, back_ref, out_ref, wave, total, counts, sem):
    copy = pltpu.make_async_copy(counts_hbm, counts, sem)
    copy.start()
    patches = counts.shape[0]
    blocks = z_ref.shape[0]
    step = 4
    upper = lax.broadcasted_iota(jnp.int32, (step, 8, LEN), 1) < 4

    def expand(i, carry):
        at = pl.multiple_of(i * step, step)
        rows = pl.ds(pl.multiple_of(i * step * 8, step * 8), step * 8)
        for half in range(2):
            def part(c):
                low = z_ref[pl.ds(at, step), 8 * c + 4 * half : 8 * c + 4 * half + 8, :]
                high = z_ref[pl.ds(at, step), 8 * c + 4 * half + 12 : 8 * c + 4 * half + 20, :]
                return jnp.where(upper, low, high).reshape(step * 8, LEN)
            growth = jnp.exp(part(0))
            angle = part(1)
            wave[half, rows, :] = growth * jnp.cos(angle)
            wave[2 + half, rows, :] = growth * jnp.sin(angle)
            total[half, rows, :] = jnp.zeros((step * 8, LEN), jnp.float32)
            total[2 + half, rows, :] = jnp.zeros((step * 8, LEN), jnp.float32)
        return carry

    lax.fori_loop(0, blocks // step, expand, 0)
    copy.wait()
    lane = lax.broadcasted_iota(jnp.int32, (LEN, LEN), 1)

    def one_group(g, carry):
        first = g * group
        exits = []
        for j in range(group):
            a = spots[first + j, 0]
            b = spots[first + j, 1]
            rows = pl.ds(a, LEN)
            keep = lane >= b
            shift = jnp.bitwise_and(LEN - b, LEN - 1)
            wr = pltpu.roll(jnp.where(keep, wave[0, rows, :], wave[1, rows, :]), shift, 1)
            wi = pltpu.roll(jnp.where(keep, wave[2, rows, :], wave[3, rows, :]), shift, 1)
            pr = probe_ref[:, :LEN]
            pi = probe_ref[:, LEN:]
            exits.append(jnp.concatenate([pr * wr - pi * wi, pr * wi + pi * wr], 1).astype(jnp.bfloat16))
        first_pass = dot(jnp.concatenate(exits, 0), ahead_ref[...]).astype(jnp.bfloat16)
        weighted = []
        for j in range(0, group, 2):
            far = dot(back_ref[...], pair_up([first_pass[k * LEN : (k + 1) * LEN] for k in (j, j + 1)]))
            for k in range(2):
                fr = far[:LEN, k * LEN : (k + 1) * LEN]
                fi = far[LEN:, k * LEN : (k + 1) * LEN]
                misfit = fr * fr + fi * fi - counts[first + j + k]
                weighted.append(jnp.concatenate([misfit * fr, misfit * fi], 1).astype(jnp.bfloat16))
        third_pass = dot(jnp.concatenate(weighted, 0), back_ref[...]).astype(jnp.bfloat16)
        for j in range(0, group, 2):
            grad = dot(ahead_ref[...], pair_up([third_pass[k * LEN : (k + 1) * LEN] for k in (j, j + 1)]))
            for k in range(2):
                a = spots[first + j + k, 0]
                b = spots[first + j + k, 1]
                rows = pl.ds(a, LEN)
                keep = lane >= jnp.bitwise_and(b, LEN - 1)
                wrap = b == LEN
                gr = grad[:LEN, k * LEN : (k + 1) * LEN]
                gi = grad[LEN:, k * LEN : (k + 1) * LEN]
                pr = probe_ref[:, :LEN]
                pi = probe_ref[:, LEN:]
                keep = lane >= b
                shift = jnp.bitwise_and(b, LEN - 1)
                ur = pltpu.roll(pr * gr + pi * gi, shift, 1)
                ui = pltpu.roll(pr * gi - pi * gr, shift, 1)
                total[0, rows, :] += jnp.where(keep, ur, 0.0)
                total[1, rows, :] += jnp.where(keep, 0.0, ur)
                total[2, rows, :] += jnp.where(keep, ui, 0.0)
                total[3, rows, :] += jnp.where(keep, 0.0, ui)
        return carry

    lax.fori_loop(0, patches // group, one_group, 0)

    def finish(i, carry):
        at = pl.multiple_of(i * step, step)
        rows = pl.ds(pl.multiple_of(i * step * 8, step * 8), step * 8)
        for half in range(2):
            orr = wave[half, rows, :]
            oi = wave[2 + half, rows, :]
            tr = total[half, rows, :]
            ti = total[2 + half, rows, :]
            for c, value in ((0, orr * tr + oi * ti), (1, orr * ti - oi * tr)):
                value = value.reshape(step, 8, LEN)
                lo = 8 * c + 4 * half
                out_ref[pl.ds(at, step), lo : lo + 4, :] = value[:, :4]
                out_ref[pl.ds(at, step), lo + 16 : lo + 20, :] = value[:, 4:]
        return carry

    lax.fori_loop(0, blocks // step, finish, 0)


def patch_gradient(z, probe, spots, counts, tables, group=GROUP):
    strips = z.shape[0]
    vmem = pl.BlockSpec(memory_space=pltpu.VMEM)
    out = pl.pallas_call(
        functools.partial(patch_kernel, group),
        out_shape=jax.ShapeDtypeStruct((strips // 2, 32, LEN), jnp.float32),
        in_specs=[pl.BlockSpec(memory_space=pltpu.SMEM), vmem, vmem, pl.BlockSpec(memory_space=pl.ANY), vmem, vmem],
        out_specs=vmem,
        scratch_shapes=[
            pltpu.VMEM((4, 4 * strips, LEN), jnp.float32),
            pltpu.VMEM((4, 4 * strips, LEN), jnp.float32),
            pltpu.VMEM(counts.shape, jnp.float32),
            pltpu.SemaphoreType.DMA,
        ],
    )(spots, z.reshape(strips // 2, 32, LEN), probe, counts, *tables)
    return out.reshape(z.shape)


def mixed(planes, spectra, out_ref):
    materials = len(planes) // 2

    def one(e, carry):
        re = jnp.zeros_like(planes[0])
        im = jnp.zeros_like(planes[0])
        for m in range(materials):
            cr = spectra[e, 2 * m]
            ci = spectra[e, 2 * m + 1]
            re = re + cr * planes[m] - ci * planes[materials + m]
            im = im + cr * planes[materials + m] + ci * planes[m]
        out_ref[e, 0:8, :] = re
        out_ref[e, 8:16, :] = im
        return carry

    lax.fori_loop(0, out_ref.shape[0], one, 0, unroll=8)


def mix_kernel(spectra, maps_ref, out_ref, rows_ref):
    for half in range(2):
        rows_ref[:, 4 * half : 4 * half + 4, :] = maps_ref[:, :, half * LEN : (half + 1) * LEN]
    mixed([rows_ref[p] for p in range(rows_ref.shape[0])], spectra, out_ref)


def unmix_kernel(factor, spectra, grads_ref, rows_ref, out_ref):
    materials = rows_ref.shape[0] // 2

    def one(e, sums):
        gr = grads_ref[e, 0:8, :]
        gi = grads_ref[e, 8:16, :]
        reals, imags = [], []
        for m in range(materials):
            cr = spectra[e, 2 * m]
            ci = spectra[e, 2 * m + 1]
            reals.append(sums[m] + cr * gr + ci * gi)
            imags.append(sums[materials + m] + cr * gi - ci * gr)
        return tuple(reals + imags)

    zero = jnp.zeros(rows_ref.shape[1:], jnp.float32)
    sums = lax.fori_loop(0, grads_ref.shape[0], one, (zero,) * (2 * materials), unroll=8)
    for p in range(2 * materials):
        out_ref[p] = rows_ref[p] - factor * sums[p]


def smooth(place, last, mine_ref, before_ref, after_ref, field):
    planes = mine_ref.shape[0]
    for j in range(3):
        lanes = slice(j * LEN, (j + 1) * LEN)
        field[:, 0:4, lanes] = before_ref[:, 4 * j : 4 * j + 4, :]
        field[:, 4:8, lanes] = mine_ref[:, 4 * j : 4 * j + 4, :]
        field[:, 8:12, lanes] = after_ref[:, 4 * j : 4 * j + 4, :]
        field[:, 12:16, lanes] = jnp.zeros((planes, 4, LEN), jnp.float32)
    shape = (16, 3 * LEN)
    row = lax.broadcasted_iota(jnp.int32, shape, 0)
    lane = lax.broadcasted_iota(jnp.int32, shape, 1)
    low_row = jnp.where(place[0] == 0, 4, 0)
    high_row = jnp.where(place[0] == last[0], 8, 16)
    low_edge = jnp.where(place[1] == last[1], 2 * LEN + LEN // 2, 0)
    high_edge = jnp.where(place[1] == 0, 2 * LEN + LEN // 2, 3 * LEN)
    inside = (row >= low_row) & (row < high_row)
    inside = inside & ((lane < 2 * LEN) | ((lane >= low_edge) & (lane < high_edge)))
    results = [None] * planes
    for m in range(planes // 2):
        pair = [field[m], field[planes // 2 + m]]
        for _ in range(TV_STEPS):
            down = [pltpu.roll(x, 15, 0) - x for x in pair]
            across = [pltpu.roll(x, 3 * LEN - 1, 1) - x for x in pair]
            square = down[0] * down[0] + across[0] * across[0] + down[1] * down[1] + across[1] * across[1]
            scale = lax.rsqrt(square + TV_EPS)
            fresh = []
            for x, d, c in zip(pair, down, across):
                d = d * scale
                c = c * scale
                moved = x + TV_STEP * (d - pltpu.roll(d, 1, 0) + c - pltpu.roll(c, 1, 1))
                fresh.append(jnp.where(inside, moved, 0.0))
            pair = fresh
        results[m], results[planes // 2 + m] = pair
    return results


def smooth_mix_kernel(last, place, spectra, mine_ref, before_ref, after_ref, rows_ref, out_ref, field):
    results = smooth(place, last, mine_ref, before_ref, after_ref, field)
    for p, value in enumerate(results):
        rows_ref[p, 0:4, :] = value[4:8, :LEN]
        rows_ref[p, 4:8, :] = value[4:8, LEN : 2 * LEN]
    mixed([rows_ref[p] for p in range(rows_ref.shape[0])], spectra, out_ref)


def smooth_kernel(last, place, mine_ref, before_ref, after_ref, out_ref, field):
    results = smooth(place, last, mine_ref, before_ref, after_ref, field)
    for p, value in enumerate(results):
        out_ref[p] = value[4:8, : 2 * LEN]


def on_chip(kernel, out_shape, scalars, arrays, scratch=()):
    vmem = pl.BlockSpec(memory_space=pltpu.VMEM)
    smem = pl.BlockSpec(memory_space=pltpu.SMEM)
    return pl.pallas_call(
        kernel,
        out_shape=out_shape,
        in_specs=[smem] * len(scalars) + [vmem] * len(arrays),
        out_specs=jax.tree.map(lambda _: vmem, out_shape),
        scratch_shapes=list(scratch),
    )(*scalars, *arrays)


def with_edges(rows):
    count = lax.axis_size("tile")
    right = [(i, i + 1) for i in range(count - 1)]
    left = [(b, a) for a, b in right]
    from_left = lax.ppermute(rows[:, 4:8], "tile", right)
    from_right = lax.ppermute(rows[:, 0:4], "tile", left)
    lane = lax.broadcasted_iota(jnp.int32, from_left.shape, 2)
    return jnp.concatenate([rows, jnp.where(lane < LEN // 2, from_right, from_left)], 1)


def from_neighbours(strip):
    count = lax.axis_size("energy")
    ahead = [(i, i + 1) for i in range(count - 1)]
    back = [(b, a) for a, b in ahead]
    return lax.ppermute(strip, "energy", ahead), lax.ppermute(strip, "energy", back)


def shards(material_maps, spectra, probes, offsets, measured):
    energies, materials, _ = spectra.shape
    planes = 2 * materials
    rows, columns = material_maps.shape[2:]
    assert rows == 4 and columns == 2 * LEN
    probe = probes[0]
    spots = offsets[0]
    counts = measured[0, 0]
    tables = dft_blocks(*dft_tables(LEN))
    weights = spectra.reshape(energies, 2 * materials)
    factor = DATA_STEP / math.sqrt(energies)
    place = jnp.stack([lax.axis_index("energy"), lax.axis_index("tile")]).astype(jnp.int32)
    last = (lax.axis_size("energy") - 1, lax.axis_size("tile") - 1)
    strip = jax.ShapeDtypeStruct((planes, 2 * rows, LEN), jnp.float32)
    spread = jax.ShapeDtypeStruct((energies, 4 * rows, LEN), jnp.float32)
    field = pltpu.VMEM((planes, 16, 3 * LEN), jnp.float32)
    maps = material_maps.reshape(planes, rows, columns)
    current = maps.reshape(planes, rows, 2, LEN).transpose(0, 2, 1, 3).reshape(planes, 2 * rows, LEN)
    mixes = on_chip(mix_kernel, spread, (weights,), (maps,), [pltpu.VMEM((planes, 2 * rows, LEN), jnp.float32)])
    for repeat in range(ITERS):
        tile = lax.all_to_all(mixes, "energy", split_axis=0, concat_axis=0, tiled=True)
        grads = patch_gradient(tile, probe, spots, counts, tables)
        grads = lax.all_to_all(grads, "energy", split_axis=0, concat_axis=0, tiled=True)
        current = on_chip(functools.partial(unmix_kernel, factor), strip, (weights,), (grads, current))
        mine = with_edges(current)
        before, after = from_neighbours(mine)
        if repeat < ITERS - 1:
            current, mixes = on_chip(
                functools.partial(smooth_mix_kernel, last), (strip, spread), (place, weights), (mine, before, after), [field]
            )
    result = jax.ShapeDtypeStruct((planes, rows, columns), jnp.float32)
    out = on_chip(functools.partial(smooth_kernel, last), result, (place,), (mine, before, after), [field])
    return out.reshape(material_maps.shape)


def solution(mesh):
    in_specs = (
        P(None, None, "energy", "tile"),
        P(),
        P("energy", None, None),
        P("tile", None, None),
        P("energy", "tile", None, None, None),
    )
    out_specs = P(None, None, "energy", "tile")
    return jax.shard_map(shards, mesh=mesh, in_specs=in_specs, out_specs=out_specs, check_vma=False)
```

```python
import functools
import math

import jax
import jax.numpy as jnp
from jax import lax
from jax.experimental import pallas as pl
from jax.experimental.pallas import tpu as pltpu
from jax.sharding import PartitionSpec as P

ITERS = 2
TV_STEPS = 3
DATA_STEP = 0.05
TV_STEP = 0.05
TV_EPS = 0.01

LEN = 128
GROUP = 8

def dft_tables(length):
    index = jnp.arange(length, dtype=jnp.int32)
    phase = index[:, None] * index[None, :] % length
    angle = phase.astype(jnp.float32) * (-2.0 * math.pi / length)
    scale = 1.0 / math.sqrt(length)
    return (
        (jnp.cos(angle) * scale).astype(jnp.bfloat16),
        (jnp.sin(angle) * scale).astype(jnp.bfloat16),
    )

def dft_blocks(fr, fi):
    ahead = jnp.concatenate([jnp.concatenate([fr, fi], 1), jnp.concatenate([-fi, fr], 1)], 0)
    back = jnp.concatenate([jnp.concatenate([fr, -fi], 1), jnp.concatenate([fi, fr], 1)], 0)
    return ahead, back

def dot(left, right):
    return jnp.dot(left, right, preferred_element_type=jnp.float32)

def pair_up(both):
    one, two = both
    return jnp.concatenate([
        jnp.concatenate([one[:, :LEN], two[:, :LEN]], 1),
        jnp.concatenate([one[:, LEN:], two[:, LEN:]], 1)], 0)

def patch_kernel(group, spots, z_ref, probe_ref, counts_hbm, ahead_ref, back_ref, out_ref, wave, total, counts, sem):
    copy = pltpu.make_async_copy(counts_hbm, counts, sem)
    copy.start()
    patches = counts.shape[0]
    blocks = z_ref.shape[0]
    step = 4
    upper = lax.broadcasted_iota(jnp.int32, (step, 8, LEN), 1) < 4

    def expand(i, carry):
        at = pl.multiple_of(i * step, step)
        rows = pl.ds(pl.multiple_of(i * step * 8, step * 8), step * 8)
        for half in range(2):
            def part(c):
                low = z_ref[pl.ds(at, step), 8 * c + 4 * half : 8 * c + 4 * half + 8, :]
                high = z_ref[pl.ds(at, step), 8 * c + 4 * half + 12 : 8 * c + 4 * half + 20, :]
                return jnp.where(upper, low, high).reshape(step * 8, LEN)
            growth = jnp.exp(part(0))
            angle = part(1)
            wave[half, rows, :] = growth * jnp.cos(angle)
            wave[2 + half, rows, :] = growth * jnp.sin(angle)
            total[half, rows, :] = jnp.zeros((step * 8, LEN), jnp.float32)
            total[2 + half, rows, :] = jnp.zeros((step * 8, LEN), jnp.float32)
        return carry

    lax.fori_loop(0, blocks // step, expand, 0)
    copy.wait()
    lane = lax.broadcasted_iota(jnp.int32, (LEN, LEN), 1)

    def one_group(g, carry):
        first = g * group
        exits = []
        for j in range(group):
            a = spots[0, first + j]
            b = spots[1, first + j]
            rows = pl.ds(a, LEN)
            keep = lane >= b
            shift = jnp.bitwise_and(LEN - b, LEN - 1)
            wr = pltpu.roll(jnp.where(keep, wave[0, rows, :], wave[1, rows, :]), shift, 1)
            wi = pltpu.roll(jnp.where(keep, wave[2, rows, :], wave[3, rows, :]), shift, 1)
            pr = probe_ref[:, :LEN]
            pi = probe_ref[:, LEN:]
            exits.append(jnp.concatenate([pr * wr - pi * wi, pr * wi + pi * wr], 1).astype(jnp.bfloat16))
        first_pass = dot(jnp.concatenate(exits, 0), ahead_ref[...]).astype(jnp.bfloat16)
        weighted = []
        for j in range(0, group, 2):
            far = dot(back_ref[...], pair_up([first_pass[k * LEN : (k + 1) * LEN] for k in (j, j + 1)]))
            for k in range(2):
                fr = far[:LEN, k * LEN : (k + 1) * LEN]
                fi = far[LEN:, k * LEN : (k + 1) * LEN]
                misfit = fr * fr + fi * fi - counts[first + j + k]
                weighted.append(jnp.concatenate([misfit * fr, misfit * fi], 1).astype(jnp.bfloat16))
        third_pass = dot(jnp.concatenate(weighted, 0), back_ref[...]).astype(jnp.bfloat16)
        for j in range(0, group, 2):
            grad = dot(ahead_ref[...], pair_up([third_pass[k * LEN : (k + 1) * LEN] for k in (j, j + 1)]))
            for k in range(2):
                a = spots[0, first + j + k]
                b = spots[1, first + j + k]
                rows = pl.ds(a, LEN)
                gr = grad[:LEN, k * LEN : (k + 1) * LEN]
                gi = grad[LEN:, k * LEN : (k + 1) * LEN]
                pr = probe_ref[:, :LEN]
                pi = probe_ref[:, LEN:]
                keep = lane >= b
                shift = jnp.bitwise_and(b, LEN - 1)
                ur = pltpu.roll(pr * gr + pi * gi, shift, 1)
                ui = pltpu.roll(pr * gi - pi * gr, shift, 1)
                total[0, rows, :] += jnp.where(keep, ur, 0.0)
                total[1, rows, :] += jnp.where(keep, 0.0, ur)
                total[2, rows, :] += jnp.where(keep, ui, 0.0)
                total[3, rows, :] += jnp.where(keep, 0.0, ui)
        return carry

    lax.fori_loop(0, patches // group, one_group, 0)

    def finish(i, carry):
        at = pl.multiple_of(i * step, step)
        rows = pl.ds(pl.multiple_of(i * step * 8, step * 8), step * 8)
        for half in range(2):
            orr = wave[half, rows, :]
            oi = wave[2 + half, rows, :]
            tr = total[half, rows, :]
            ti = total[2 + half, rows, :]
            for c, value in ((0, orr * tr + oi * ti), (1, orr * ti - oi * tr)):
                value = value.reshape(step, 8, LEN)
                lo = 8 * c + 4 * half
                out_ref[pl.ds(at, step), lo : lo + 4, :] = value[:, :4]
                out_ref[pl.ds(at, step), lo + 16 : lo + 20, :] = value[:, 4:]
        return carry

    lax.fori_loop(0, blocks // step, finish, 0)


def patch_gradient(z, probe, spots, counts, tables, group=GROUP):
    strips = z.shape[0]
    vmem = pl.BlockSpec(memory_space=pltpu.VMEM)
    out = pl.pallas_call(
        functools.partial(patch_kernel, group),
        out_shape=jax.ShapeDtypeStruct((strips // 2, 32, LEN), jnp.float32),
        in_specs=[pl.BlockSpec(memory_space=pltpu.SMEM), vmem, vmem, pl.BlockSpec(memory_space=pl.ANY), vmem, vmem],
        out_specs=vmem,
        scratch_shapes=[
            pltpu.VMEM((4, 4 * strips, LEN), jnp.float32),
            pltpu.VMEM((4, 4 * strips, LEN), jnp.float32),
            pltpu.VMEM(counts.shape, jnp.float32),
            pltpu.SemaphoreType.DMA,
        ],
        compiler_params=pltpu.CompilerParams(vmem_limit_bytes=16 << 20),
    )(spots, z.reshape(strips // 2, 32, LEN), probe, counts, *tables)
    return out.reshape(z.shape)


def mixed(planes, spectra, out_ref):
    materials = len(planes) // 2

    def one(e, carry):
        re = jnp.zeros_like(planes[0])
        im = jnp.zeros_like(planes[0])
        for m in range(materials):
            cr = spectra[2 * m, e]
            ci = spectra[2 * m + 1, e]
            re = re + cr * planes[m] - ci * planes[materials + m]
            im = im + cr * planes[materials + m] + ci * planes[m]
        out_ref[e, 0:8, :] = re
        out_ref[e, 8:16, :] = im
        return carry

    lax.fori_loop(0, out_ref.shape[0], one, 0, unroll=8)


def mix_kernel(spectra, maps_ref, out_ref, rows_ref):
    for half in range(2):
        rows_ref[:, 4 * half : 4 * half + 4, :] = maps_ref[:, :, half * LEN : (half + 1) * LEN]
    mixed([rows_ref[p] for p in range(rows_ref.shape[0])], spectra, out_ref)


def unmix_kernel(factor, spectra, grads_ref, rows_ref, out_ref, low_ref, high_ref):
    materials = rows_ref.shape[0] // 2

    def one(e, sums):
        gr = grads_ref[e, 0:8, :]
        gi = grads_ref[e, 8:16, :]
        reals, imags = [], []
        for m in range(materials):
            cr = spectra[2 * m, e]
            ci = spectra[2 * m + 1, e]
            reals.append(sums[m] + cr * gr + ci * gi)
            imags.append(sums[materials + m] + cr * gi - ci * gr)
        return tuple(reals + imags)

    zero = jnp.zeros(rows_ref.shape[1:], jnp.float32)
    sums = lax.fori_loop(0, grads_ref.shape[0], one, (zero,) * (2 * materials), unroll=8)
    for p in range(2 * materials):
        value = rows_ref[p] - factor * sums[p]
        out_ref[p] = value
        low_ref[p] = value[:4]
        high_ref[p] = value[4:]


def smooth(place, last, mine_ref, before_ref, after_ref, field):
    planes = mine_ref.shape[0]
    for j in range(3):
        lanes = slice(j * LEN, (j + 1) * LEN)
        field[:, 0:4, lanes] = before_ref[:, 4 * j : 4 * j + 4, :]
        field[:, 4:8, lanes] = mine_ref[:, 4 * j : 4 * j + 4, :]
        field[:, 8:12, lanes] = after_ref[:, 4 * j : 4 * j + 4, :]
        field[:, 12:16, lanes] = jnp.zeros((planes, 4, LEN), jnp.float32)
    shape = (16, 3 * LEN)
    row = lax.broadcasted_iota(jnp.int32, shape, 0)
    lane = lax.broadcasted_iota(jnp.int32, shape, 1)
    low_row = jnp.where(place[0] == 0, 4, 0)
    high_row = jnp.where(place[0] == last[0], 8, 16)
    low_edge = jnp.where(place[1] == last[1], 2 * LEN + LEN // 2, 0)
    high_edge = jnp.where(place[1] == 0, 2 * LEN + LEN // 2, 3 * LEN)
    inside = (row >= low_row) & (row < high_row)
    inside = inside & ((lane < 2 * LEN) | ((lane >= low_edge) & (lane < high_edge)))
    results = [None] * planes
    for m in range(planes // 2):
        pair = [jnp.where(inside, field[p], 0.0) for p in (m, planes // 2 + m)]
        for _ in range(TV_STEPS):
            down = [pltpu.roll(x, 15, 0) - x for x in pair]
            across = [pltpu.roll(x, 3 * LEN - 1, 1) - x for x in pair]
            square = down[0] * down[0] + across[0] * across[0] + down[1] * down[1] + across[1] * across[1]
            scale = lax.rsqrt(square + TV_EPS)
            fresh = []
            for x, d, c in zip(pair, down, across):
                d = d * scale
                c = c * scale
                moved = x + TV_STEP * (d - pltpu.roll(d, 1, 0) + c - pltpu.roll(c, 1, 1))
                fresh.append(jnp.where(inside, moved, 0.0))
            pair = fresh
        results[m], results[planes // 2 + m] = pair
    return results


def smooth_mix_kernel(last, place, spectra, mine_ref, before_ref, after_ref, rows_ref, out_ref, field):
    results = smooth(place, last, mine_ref, before_ref, after_ref, field)
    for p, value in enumerate(results):
        rows_ref[p, 0:4, :] = value[4:8, :LEN]
        rows_ref[p, 4:8, :] = value[4:8, LEN : 2 * LEN]
    mixed([rows_ref[p] for p in range(rows_ref.shape[0])], spectra, out_ref)


def smooth_kernel(last, place, mine_ref, before_ref, after_ref, out_ref, field):
    results = smooth(place, last, mine_ref, before_ref, after_ref, field)
    for p, value in enumerate(results):
        out_ref[p] = value[4:8, : 2 * LEN]


def on_chip(kernel, out_shape, scalars, arrays, scratch=()):
    vmem = pl.BlockSpec(memory_space=pltpu.VMEM)
    smem = pl.BlockSpec(memory_space=pltpu.SMEM)
    return pl.pallas_call(
        kernel,
        out_shape=out_shape,
        in_specs=[smem] * len(scalars) + [vmem] * len(arrays),
        out_specs=jax.tree.map(lambda _: vmem, out_shape),
        scratch_shapes=list(scratch),
        compiler_params=pltpu.CompilerParams(vmem_limit_bytes=8 << 20),
    )(*scalars, *arrays)


def ring(axis):
    count = lax.axis_size(axis)
    ahead = [(i, (i + 1) % count) for i in range(count)]
    return ahead, [(b, a) for a, b in ahead]


def with_edges(rows, low, high):
    ahead, back = ring("tile")
    from_left = lax.ppermute(high, "tile", ahead)
    from_right = lax.ppermute(low, "tile", back)
    lane = lax.broadcasted_iota(jnp.int32, from_left.shape, 2)
    return jnp.concatenate([rows, jnp.where(lane < LEN // 2, from_right, from_left)], 1)


def from_neighbours(strip):
    ahead, back = ring("energy")
    return lax.ppermute(strip, "energy", ahead), lax.ppermute(strip, "energy", back)


def shards(material_maps, spectra, probes, offsets, measured):
    energies, materials, _ = spectra.shape
    planes = 2 * materials
    rows, columns = material_maps.shape[2:]
    assert rows == 4 and columns == 2 * LEN
    probe = probes[0]
    spots = offsets[0].T
    counts = measured[0, 0]
    tables = dft_blocks(*dft_tables(LEN))
    weights = spectra.transpose(1, 2, 0).reshape(2 * materials, energies)
    factor = DATA_STEP / math.sqrt(energies)
    place = jnp.stack([lax.axis_index("energy"), lax.axis_index("tile")]).astype(jnp.int32)
    last = (lax.axis_size("energy") - 1, lax.axis_size("tile") - 1)
    strip = jax.ShapeDtypeStruct((planes, 2 * rows, LEN), jnp.float32)
    part = jax.ShapeDtypeStruct((planes, rows, LEN), jnp.float32)
    spread = jax.ShapeDtypeStruct((energies, 4 * rows, LEN), jnp.float32)
    field = pltpu.VMEM((planes, 16, 3 * LEN), jnp.float32)
    maps = material_maps.reshape(planes, rows, columns)
    current = maps.reshape(planes, rows, 2, LEN).transpose(0, 2, 1, 3).reshape(planes, 2 * rows, LEN)
    mixes = on_chip(mix_kernel, spread, (weights,), (maps,), [pltpu.VMEM((planes, 2 * rows, LEN), jnp.float32)])
    for repeat in range(ITERS):
        tile = lax.all_to_all(mixes, "energy", split_axis=0, concat_axis=0, tiled=True)
        grads = patch_gradient(tile, probe, spots, counts, tables)
        grads = lax.all_to_all(grads, "energy", split_axis=0, concat_axis=0, tiled=True)
        current, low, high = on_chip(
            functools.partial(unmix_kernel, factor), (strip, part, part), (weights,), (grads, current)
        )
        mine = with_edges(current, low, high)
        before, after = from_neighbours(mine)
        if repeat < ITERS - 1:
            current, mixes = on_chip(
                functools.partial(smooth_mix_kernel, last), (strip, spread), (place, weights), (mine, before, after), [field]
            )
    result = jax.ShapeDtypeStruct((planes, rows, columns), jnp.float32)
    out = on_chip(functools.partial(smooth_kernel, last), result, (place,), (mine, before, after), [field])
    return out.reshape(material_maps.shape)


def solution(mesh):
    in_specs = (
        P(None, None, "energy", "tile"),
        P(),
        P("energy", None, None),
        P("tile", None, None),
        P("energy", "tile", None, None, None),
    )
    out_specs = P(None, None, "energy", "tile")
    return jax.shard_map(shards, mesh=mesh, in_specs=in_specs, out_specs=out_specs, check_vma=False)
```

```python
import functools
import math

import jax
import jax.numpy as jnp
import numpy as np
from jax import lax
from jax.experimental import pallas as pl
from jax.experimental.pallas import tpu as pltpu
from jax.sharding import PartitionSpec as P

ITERS = 2
TV_STEPS = 3
DATA_STEP = 0.05
TV_STEP = 0.05
TV_EPS = 0.01

LEN = 128
GROUP = 16
LIMIT = 4096.0

def dft_tables(length):
    index = np.arange(length)
    angle = (index[:, None] * index[None, :] % length) * (-2.0 * math.pi / length)
    scale = 1.0 / math.sqrt(length)
    return tuple((wave(angle) * scale).astype(np.float32).astype(jnp.bfloat16) for wave in (np.cos, np.sin))


def dft_blocks(fr, fi):
    ahead = np.block([[fr, fi], [-fi, fr]])
    back = np.block([[fr, -fi], [fi, fr]])
    return jnp.asarray(ahead), jnp.asarray(back)


def dot(left, right):
    return jnp.dot(left, right, preferred_element_type=jnp.float32)

def pair_up(both):
    one, two = both
    return jnp.concatenate([
        jnp.concatenate([one[:, :LEN], two[:, :LEN]], 1),
        jnp.concatenate([one[:, LEN:], two[:, LEN:]], 1)], 0)

def sine_cosine(angle):
    turns = jnp.floor(angle * (2.0 / math.pi) + 0.5)
    rest = ((angle - turns * 1.5703125) - turns * 4.837512969970703125e-4) - turns * 7.54978995489188216e-8
    quadrant = turns.astype(jnp.int32)
    square = rest * rest
    sine = ((-1.9515295891e-4 * square + 8.3321608736e-3) * square - 1.6666654611e-1) * square * rest + rest
    cosine = ((2.443315711809948e-5 * square - 1.388731625493765e-3) * square + 4.166664568298827e-2) * square * square
    cosine = cosine - 0.5 * square + 1.0
    odd = (quadrant & 1) == 1
    first = jnp.where(odd, cosine, sine)
    second = jnp.where(odd, sine, cosine)
    return (
        jnp.where((quadrant & 2) == 2, -first, first),
        jnp.where(((quadrant + 1) & 2) == 2, -second, second),
    )


def patch_kernel(
    group, z_ref, spots_hbm, counts_hbm, probe_hbm, ahead_hbm, back_hbm, out_ref,
    wave, total, spots, counts, probe_ref, ahead_ref, back_ref, sems
):
    copies = [
        pltpu.make_async_copy(source, target, sems.at[i])
        for i, (source, target) in enumerate(
            (
                (spots_hbm, spots),
                (counts_hbm, counts),
                (probe_hbm, probe_ref),
                (ahead_hbm, ahead_ref),
                (back_hbm, back_ref),
            )
        )
    ]
    for copy in copies:
        copy.start()
    patches = counts.shape[0]
    blocks = z_ref.shape[0]
    step = 4
    upper = lax.broadcasted_iota(jnp.int32, (step, 8, LEN), 1) < 4

    def parts(i, half):
        at = pl.multiple_of(i * step, step)
        rows = pl.ds(pl.multiple_of(i * step * 8, step * 8), step * 8)

        def part(c):
            low = z_ref[pl.ds(at, step), 8 * c + 4 * half : 8 * c + 4 * half + 8, :]
            high = z_ref[pl.ds(at, step), 8 * c + 4 * half + 12 : 8 * c + 4 * half + 20, :]
            return jnp.where(upper, low, high).reshape(step * 8, LEN)

        return rows, part(0), part(1)

    def expand(i, largest):
        for half in range(2):
            rows, size, angle = parts(i, half)
            growth = jnp.exp(size)
            sine, cosine = sine_cosine(angle)
            wave[half, rows, :] = growth * cosine
            wave[2 + half, rows, :] = growth * sine
            total[half, rows, :] = jnp.zeros((step * 8, LEN), jnp.float32)
            total[2 + half, rows, :] = jnp.zeros((step * 8, LEN), jnp.float32)
            largest = jnp.maximum(largest, jnp.abs(angle))
        return largest

    largest = lax.fori_loop(0, blocks // step, expand, jnp.zeros((step * 8, LEN), jnp.float32))

    @pl.when(jnp.max(largest) > LIMIT)
    def _():
        def again(i, carry):
            for half in range(2):
                rows, size, angle = parts(i, half)
                growth = jnp.exp(size)
                wave[half, rows, :] = growth * jnp.cos(angle)
                wave[2 + half, rows, :] = growth * jnp.sin(angle)
            return carry

        lax.fori_loop(0, blocks // step, again, 0)

    for copy in copies:
        copy.wait()
    lane = lax.broadcasted_iota(jnp.int32, (LEN, LEN), 1)

    def one_group(g, carry):
        first = g * group
        exits = []
        for j in range(group):
            a = spots[0, first + j]
            b = spots[1, first + j]
            rows = pl.ds(a, LEN)
            keep = lane >= b
            shift = jnp.bitwise_and(LEN - b, LEN - 1)
            wr = pltpu.roll(jnp.where(keep, wave[0, rows, :], wave[1, rows, :]), shift, 1)
            wi = pltpu.roll(jnp.where(keep, wave[2, rows, :], wave[3, rows, :]), shift, 1)
            pr = probe_ref[:, :LEN]
            pi = probe_ref[:, LEN:]
            exits.append(jnp.concatenate([pr * wr - pi * wi, pr * wi + pi * wr], 1).astype(jnp.bfloat16))
        first_pass = dot(jnp.concatenate(exits, 0), ahead_ref[...]).astype(jnp.bfloat16)
        weighted = []
        for j in range(0, group, 2):
            far = dot(back_ref[...], pair_up([first_pass[k * LEN : (k + 1) * LEN] for k in (j, j + 1)]))
            for k in range(2):
                fr = far[:LEN, k * LEN : (k + 1) * LEN]
                fi = far[LEN:, k * LEN : (k + 1) * LEN]
                misfit = fr * fr + fi * fi - counts[first + j + k]
                weighted.append(jnp.concatenate([misfit * fr, misfit * fi], 1).astype(jnp.bfloat16))
        third_pass = dot(jnp.concatenate(weighted, 0), back_ref[...]).astype(jnp.bfloat16)
        for j in range(0, group, 2):
            grad = dot(ahead_ref[...], pair_up([third_pass[k * LEN : (k + 1) * LEN] for k in (j, j + 1)]))
            for k in range(2):
                a = spots[0, first + j + k]
                b = spots[1, first + j + k]
                rows = pl.ds(a, LEN)
                gr = grad[:LEN, k * LEN : (k + 1) * LEN]
                gi = grad[LEN:, k * LEN : (k + 1) * LEN]
                pr = probe_ref[:, :LEN]
                pi = probe_ref[:, LEN:]
                keep = lane >= b
                shift = jnp.bitwise_and(b, LEN - 1)
                ur = pltpu.roll(pr * gr + pi * gi, shift, 1)
                ui = pltpu.roll(pr * gi - pi * gr, shift, 1)
                total[0, rows, :] += jnp.where(keep, ur, 0.0)
                total[1, rows, :] += jnp.where(keep, 0.0, ur)
                total[2, rows, :] += jnp.where(keep, ui, 0.0)
                total[3, rows, :] += jnp.where(keep, 0.0, ui)
        return carry

    lax.fori_loop(0, patches // group, one_group, 0)

    def finish(i, carry):
        at = pl.multiple_of(i * step, step)
        rows = pl.ds(pl.multiple_of(i * step * 8, step * 8), step * 8)
        for half in range(2):
            orr = wave[half, rows, :]
            oi = wave[2 + half, rows, :]
            tr = total[half, rows, :]
            ti = total[2 + half, rows, :]
            for c, value in ((0, orr * tr + oi * ti), (1, orr * ti - oi * tr)):
                value = value.reshape(step, 8, LEN)
                lo = 8 * c + 4 * half
                out_ref[pl.ds(at, step), lo : lo + 4, :] = value[:, :4]
                out_ref[pl.ds(at, step), lo + 16 : lo + 20, :] = value[:, 4:]
        return carry

    lax.fori_loop(0, blocks // step, finish, 0)


def stay(array):
    return pltpu.with_memory_space_constraint(array, pltpu.HBM)


def patch_gradient(z, probe, spots, counts, tables, group=GROUP):
    strips = z.shape[0]
    vmem = pl.BlockSpec(memory_space=pltpu.VMEM)
    hbm = pl.BlockSpec(memory_space=pltpu.HBM)
    out = pl.pallas_call(
        functools.partial(patch_kernel, group),
        out_shape=jax.ShapeDtypeStruct((strips // 2, 32, LEN), jnp.float32),
        in_specs=[vmem] + [hbm] * 5,
        out_specs=vmem,
        scratch_shapes=[
            pltpu.VMEM((4, 4 * strips, LEN), jnp.float32),
            pltpu.VMEM((4, 4 * strips, LEN), jnp.float32),
            pltpu.SMEM(spots.shape, jnp.int32),
            pltpu.VMEM(counts.shape, jnp.float32),
            pltpu.VMEM(probe.shape, jnp.float32),
            pltpu.VMEM((2 * LEN, 2 * LEN), jnp.bfloat16),
            pltpu.VMEM((2 * LEN, 2 * LEN), jnp.bfloat16),
            pltpu.SemaphoreType.DMA((5,)),
        ],
        compiler_params=pltpu.CompilerParams(vmem_limit_bytes=16 << 20),
    )(z.reshape(strips // 2, 32, LEN), *[stay(x) for x in (spots, counts, probe, *tables)])
    return out.reshape(z.shape)


def mixed(planes, spectra, out_ref):
    materials = len(planes) // 2

    def one(e, carry):
        re = jnp.zeros_like(planes[0])
        im = jnp.zeros_like(planes[0])
        for m in range(materials):
            cr = spectra[2 * m, e]
            ci = spectra[2 * m + 1, e]
            re = re + cr * planes[m] - ci * planes[materials + m]
            im = im + cr * planes[materials + m] + ci * planes[m]
        out_ref[e, 0:8, :] = re
        out_ref[e, 8:16, :] = im
        return carry

    lax.fori_loop(0, out_ref.shape[0], one, 0, unroll=8)


def mix_kernel(spectra_hbm, maps_hbm, out_ref, maps, rows_ref, spectra, sems):
    copies = [
        pltpu.make_async_copy(spectra_hbm, spectra, sems.at[0]),
        pltpu.make_async_copy(maps_hbm, maps, sems.at[1]),
    ]
    for copy in copies:
        copy.start()
    for copy in copies:
        copy.wait()
    for half in range(2):
        rows_ref[:, 4 * half : 4 * half + 4, :] = maps[:, :, half * LEN : (half + 1) * LEN]
    mixed([rows_ref[p] for p in range(rows_ref.shape[0])], spectra, out_ref)


def unmix_kernel(factor, spectra, grads_ref, rows_ref, out_ref, low_ref, high_ref):
    materials = rows_ref.shape[0] // 2

    def one(e, sums):
        gr = grads_ref[e, 0:8, :]
        gi = grads_ref[e, 8:16, :]
        reals, imags = [], []
        for m in range(materials):
            cr = spectra[2 * m, e]
            ci = spectra[2 * m + 1, e]
            reals.append(sums[m] + cr * gr + ci * gi)
            imags.append(sums[materials + m] + cr * gi - ci * gr)
        return tuple(reals + imags)

    zero = jnp.zeros(rows_ref.shape[1:], jnp.float32)
    sums = lax.fori_loop(0, grads_ref.shape[0], one, (zero,) * (2 * materials), unroll=8)
    for p in range(2 * materials):
        value = rows_ref[p] - factor * sums[p]
        out_ref[p] = value
        low_ref[p] = value[:4]
        high_ref[p] = value[4:]


def smooth(place, last, mine_ref, before_ref, after_ref, field):
    planes = mine_ref.shape[0]
    for j in range(3):
        lanes = slice(j * LEN, (j + 1) * LEN)
        field[:, 0:4, lanes] = before_ref[:, 4 * j : 4 * j + 4, :]
        field[:, 4:8, lanes] = mine_ref[:, 4 * j : 4 * j + 4, :]
        field[:, 8:12, lanes] = after_ref[:, 4 * j : 4 * j + 4, :]
        field[:, 12:16, lanes] = jnp.zeros((planes, 4, LEN), jnp.float32)
    shape = (16, 3 * LEN)
    row = lax.broadcasted_iota(jnp.int32, shape, 0)
    lane = lax.broadcasted_iota(jnp.int32, shape, 1)
    low_row = jnp.where(place[0] == 0, 4, 0)
    high_row = jnp.where(place[0] == last[0], 8, 16)
    low_edge = jnp.where(place[1] == last[1], 2 * LEN + LEN // 2, 0)
    high_edge = jnp.where(place[1] == 0, 2 * LEN + LEN // 2, 3 * LEN)
    inside = (row >= low_row) & (row < high_row)
    inside = inside & ((lane < 2 * LEN) | ((lane >= low_edge) & (lane < high_edge)))
    results = [None] * planes
    for m in range(planes // 2):
        pair = [jnp.where(inside, field[p], 0.0) for p in (m, planes // 2 + m)]
        for _ in range(TV_STEPS):
            down = [pltpu.roll(x, 15, 0) - x for x in pair]
            across = [pltpu.roll(x, 3 * LEN - 1, 1) - x for x in pair]
            square = down[0] * down[0] + across[0] * across[0] + down[1] * down[1] + across[1] * across[1]
            scale = lax.rsqrt(square + TV_EPS)
            fresh = []
            for x, d, c in zip(pair, down, across):
                d = d * scale
                c = c * scale
                moved = x + TV_STEP * (d - pltpu.roll(d, 1, 0) + c - pltpu.roll(c, 1, 1))
                fresh.append(jnp.where(inside, moved, 0.0))
            pair = fresh
        results[m], results[planes // 2 + m] = pair
    return results


def smooth_mix_kernel(last, place, spectra, mine_ref, before_ref, after_ref, rows_ref, out_ref, field):
    results = smooth(place, last, mine_ref, before_ref, after_ref, field)
    for p, value in enumerate(results):
        rows_ref[p, 0:4, :] = value[4:8, :LEN]
        rows_ref[p, 4:8, :] = value[4:8, LEN : 2 * LEN]
    mixed([rows_ref[p] for p in range(rows_ref.shape[0])], spectra, out_ref)


def smooth_kernel(last, place, mine_ref, before_ref, after_ref, out_ref, field):
    results = smooth(place, last, mine_ref, before_ref, after_ref, field)
    for p, value in enumerate(results):
        out_ref[p] = value[4:8, : 2 * LEN]


def on_chip(kernel, out_shape, scalars, arrays, scratch=()):
    vmem = pl.BlockSpec(memory_space=pltpu.VMEM)
    smem = pl.BlockSpec(memory_space=pltpu.SMEM)
    return pl.pallas_call(
        kernel,
        out_shape=out_shape,
        in_specs=[smem] * len(scalars) + [vmem] * len(arrays),
        out_specs=jax.tree.map(lambda _: vmem, out_shape),
        scratch_shapes=list(scratch),
        compiler_params=pltpu.CompilerParams(vmem_limit_bytes=8 << 20),
    )(*scalars, *arrays)


def ring(axis):
    count = lax.axis_size(axis)
    ahead = [(i, (i + 1) % count) for i in range(count)]
    return ahead, [(b, a) for a, b in ahead]


def with_edges(rows, low, high):
    ahead, back = ring("tile")
    from_left = lax.ppermute(high, "tile", ahead)
    from_right = lax.ppermute(low, "tile", back)
    lane = lax.broadcasted_iota(jnp.int32, from_left.shape, 2)
    return jnp.concatenate([rows, jnp.where(lane < LEN // 2, from_right, from_left)], 1)


def from_neighbours(strip):
    ahead, back = ring("energy")
    return lax.ppermute(strip, "energy", ahead), lax.ppermute(strip, "energy", back)


def shards(material_maps, spectra, probes, offsets, measured):
    energies, materials, _ = spectra.shape
    planes = 2 * materials
    rows, columns = material_maps.shape[2:]
    assert rows == 4 and columns == 2 * LEN
    probe = probes[0]
    spots = offsets[0].T
    counts = measured[0, 0]
    tables = dft_blocks(*dft_tables(LEN))
    weights = spectra.transpose(1, 2, 0).reshape(2 * materials, energies)
    factor = DATA_STEP / math.sqrt(energies)
    place = jnp.stack([lax.axis_index("energy"), lax.axis_index("tile")]).astype(jnp.int32)
    last = (lax.axis_size("energy") - 1, lax.axis_size("tile") - 1)
    strip = jax.ShapeDtypeStruct((planes, 2 * rows, LEN), jnp.float32)
    part = jax.ShapeDtypeStruct((planes, rows, LEN), jnp.float32)
    spread = jax.ShapeDtypeStruct((energies, 4 * rows, LEN), jnp.float32)
    field = pltpu.VMEM((planes, 16, 3 * LEN), jnp.float32)
    maps = material_maps.reshape(planes, rows, columns)
    current = maps.reshape(planes, rows, 2, LEN).transpose(0, 2, 1, 3).reshape(planes, 2 * rows, LEN)
    hbm = pl.BlockSpec(memory_space=pltpu.HBM)
    mixes = pl.pallas_call(
        mix_kernel,
        out_shape=spread,
        in_specs=[hbm, hbm],
        out_specs=pl.BlockSpec(memory_space=pltpu.VMEM),
        scratch_shapes=[
            pltpu.VMEM(maps.shape, jnp.float32),
            pltpu.VMEM(strip.shape, jnp.float32),
            pltpu.SMEM(weights.shape, jnp.float32),
            pltpu.SemaphoreType.DMA((2,)),
        ],
        compiler_params=pltpu.CompilerParams(vmem_limit_bytes=8 << 20),
    )(stay(weights), stay(maps))
    for repeat in range(ITERS):
        tile = lax.all_to_all(mixes, "energy", split_axis=0, concat_axis=0, tiled=True)
        grads = patch_gradient(tile, probe, spots, counts, tables)
        grads = lax.all_to_all(grads, "energy", split_axis=0, concat_axis=0, tiled=True)
        current, low, high = on_chip(
            functools.partial(unmix_kernel, factor), (strip, part, part), (weights,), (grads, current)
        )
        mine = with_edges(current, low, high)
        before, after = from_neighbours(mine)
        if repeat < ITERS - 1:
            current, mixes = on_chip(
                functools.partial(smooth_mix_kernel, last), (strip, spread), (place, weights), (mine, before, after), [field]
            )
    result = jax.ShapeDtypeStruct((planes, rows, columns), jnp.float32)
    out = on_chip(functools.partial(smooth_kernel, last), result, (place,), (mine, before, after), [field])
    return out.reshape(material_maps.shape)


def solution(mesh):
    in_specs = (
        P(None, None, "energy", "tile"),
        P(),
        P("energy", None, None),
        P("tile", None, None),
        P("energy", "tile", None, None, None),
    )
    out_specs = P(None, None, "energy", "tile")
    return jax.shard_map(shards, mesh=mesh, in_specs=in_specs, out_specs=out_specs, check_vma=False)
```

```python
import functools
import math

import jax
import jax.numpy as jnp
import numpy as np
from jax import lax
from jax.experimental import pallas as pl
from jax.experimental.pallas import tpu as pltpu
from jax.sharding import PartitionSpec as P

ITERS = 2
TV_STEPS = 3
DATA_STEP = 0.05
TV_STEP = 0.05
TV_EPS = 0.01

LEN = 128
GROUP = 16
LIMIT = 4096.0

def dft_tables(length):
    index = np.arange(length)
    angle = (index[:, None] * index[None, :] % length) * (-2.0 * math.pi / length)
    scale = 1.0 / math.sqrt(length)
    return tuple((wave(angle) * scale).astype(np.float32).astype(jnp.bfloat16) for wave in (np.cos, np.sin))


def dft_blocks(fr, fi):
    ahead = np.block([[fr, fi], [-fi, fr]])
    back = np.block([[fr, -fi], [fi, fr]])
    return jnp.asarray(ahead), jnp.asarray(back)


def dot(left, right):
    return jnp.dot(left, right, preferred_element_type=jnp.float32)

def pair_up(both):
    one, two = both
    return jnp.concatenate([
        jnp.concatenate([one[:, :LEN], two[:, :LEN]], 1),
        jnp.concatenate([one[:, LEN:], two[:, LEN:]], 1)], 0)

def sine_cosine(angle):
    turns = jnp.floor(angle * (2.0 / math.pi) + 0.5)
    rest = ((angle - turns * 1.5703125) - turns * 4.837512969970703125e-4) - turns * 7.54978995489188216e-8
    quadrant = turns.astype(jnp.int32)
    square = rest * rest
    sine = ((-1.9515295891e-4 * square + 8.3321608736e-3) * square - 1.6666654611e-1) * square * rest + rest
    cosine = ((2.443315711809948e-5 * square - 1.388731625493765e-3) * square + 4.166664568298827e-2) * square * square
    cosine = cosine - 0.5 * square + 1.0
    odd = (quadrant & 1) == 1
    first = jnp.where(odd, cosine, sine)
    second = jnp.where(odd, sine, cosine)
    return (
        jnp.where((quadrant & 2) == 2, -first, first),
        jnp.where(((quadrant + 1) & 2) == 2, -second, second),
    )


def patch_kernel(
    group, z_ref, spots_hbm, counts_from, probe_from, ahead_from, back_from, out_ref, wave, total, spots, *rest
):
    *buffers, sems = rest
    sources = (counts_from, probe_from, ahead_from, back_from)
    counts, probe_ref, ahead_ref, back_ref = buffers or sources
    moves = [(spots_hbm, spots), *zip(sources, buffers)]
    copies = [pltpu.make_async_copy(source, target, sems.at[i]) for i, (source, target) in enumerate(moves)]
    for copy in copies:
        copy.start()
    patches = counts.shape[0]
    blocks = z_ref.shape[0]
    step = 4
    upper = lax.broadcasted_iota(jnp.int32, (step, 8, LEN), 1) < 4

    def parts(i, half):
        at = pl.multiple_of(i * step, step)
        rows = pl.ds(pl.multiple_of(i * step * 8, step * 8), step * 8)

        def part(c):
            low = z_ref[pl.ds(at, step), 8 * c + 4 * half : 8 * c + 4 * half + 8, :]
            high = z_ref[pl.ds(at, step), 8 * c + 4 * half + 12 : 8 * c + 4 * half + 20, :]
            return jnp.where(upper, low, high).reshape(step * 8, LEN)

        return rows, part(0), part(1)

    def expand(i, largest):
        for half in range(2):
            rows, size, angle = parts(i, half)
            growth = jnp.exp(size)
            sine, cosine = sine_cosine(angle)
            wave[half, rows, :] = growth * cosine
            wave[2 + half, rows, :] = growth * sine
            total[half, rows, :] = jnp.zeros((step * 8, LEN), jnp.float32)
            total[2 + half, rows, :] = jnp.zeros((step * 8, LEN), jnp.float32)
            largest = jnp.maximum(largest, jnp.abs(angle))
        return largest

    largest = lax.fori_loop(0, blocks // step, expand, jnp.zeros((step * 8, LEN), jnp.float32))

    @pl.when(jnp.max(largest) > LIMIT)
    def _():
        def again(i, carry):
            for half in range(2):
                rows, size, angle = parts(i, half)
                growth = jnp.exp(size)
                wave[half, rows, :] = growth * jnp.cos(angle)
                wave[2 + half, rows, :] = growth * jnp.sin(angle)
            return carry

        lax.fori_loop(0, blocks // step, again, 0)

    for copy in copies:
        copy.wait()
    lane = lax.broadcasted_iota(jnp.int32, (LEN, LEN), 1)

    def one_group(g, carry):
        first = g * group
        exits = []
        for j in range(group):
            a = spots[0, first + j]
            b = spots[1, first + j]
            rows = pl.ds(a, LEN)
            keep = lane >= b
            shift = jnp.bitwise_and(LEN - b, LEN - 1)
            wr = pltpu.roll(jnp.where(keep, wave[0, rows, :], wave[1, rows, :]), shift, 1)
            wi = pltpu.roll(jnp.where(keep, wave[2, rows, :], wave[3, rows, :]), shift, 1)
            pr = probe_ref[:, :LEN]
            pi = probe_ref[:, LEN:]
            exits.append(jnp.concatenate([pr * wr - pi * wi, pr * wi + pi * wr], 1).astype(jnp.bfloat16))
        first_pass = dot(jnp.concatenate(exits, 0), ahead_ref[...]).astype(jnp.bfloat16)
        weighted = []
        for j in range(0, group, 2):
            far = dot(back_ref[...], pair_up([first_pass[k * LEN : (k + 1) * LEN] for k in (j, j + 1)]))
            for k in range(2):
                fr = far[:LEN, k * LEN : (k + 1) * LEN]
                fi = far[LEN:, k * LEN : (k + 1) * LEN]
                misfit = fr * fr + fi * fi - counts[first + j + k]
                weighted.append(jnp.concatenate([misfit * fr, misfit * fi], 1).astype(jnp.bfloat16))
        third_pass = dot(jnp.concatenate(weighted, 0), back_ref[...]).astype(jnp.bfloat16)
        for j in range(0, group, 2):
            grad = dot(ahead_ref[...], pair_up([third_pass[k * LEN : (k + 1) * LEN] for k in (j, j + 1)]))
            for k in range(2):
                a = spots[0, first + j + k]
                b = spots[1, first + j + k]
                rows = pl.ds(a, LEN)
                gr = grad[:LEN, k * LEN : (k + 1) * LEN]
                gi = grad[LEN:, k * LEN : (k + 1) * LEN]
                pr = probe_ref[:, :LEN]
                pi = probe_ref[:, LEN:]
                keep = lane >= b
                shift = jnp.bitwise_and(b, LEN - 1)
                ur = pltpu.roll(pr * gr + pi * gi, shift, 1)
                ui = pltpu.roll(pr * gi - pi * gr, shift, 1)
                total[0, rows, :] += jnp.where(keep, ur, 0.0)
                total[1, rows, :] += jnp.where(keep, 0.0, ur)
                total[2, rows, :] += jnp.where(keep, ui, 0.0)
                total[3, rows, :] += jnp.where(keep, 0.0, ui)
        return carry

    lax.fori_loop(0, patches // group, one_group, 0)

    def finish(i, carry):
        at = pl.multiple_of(i * step, step)
        rows = pl.ds(pl.multiple_of(i * step * 8, step * 8), step * 8)
        for half in range(2):
            orr = wave[half, rows, :]
            oi = wave[2 + half, rows, :]
            tr = total[half, rows, :]
            ti = total[2 + half, rows, :]
            for c, value in ((0, orr * tr + oi * ti), (1, orr * ti - oi * tr)):
                value = value.reshape(step, 8, LEN)
                lo = 8 * c + 4 * half
                out_ref[pl.ds(at, step), lo : lo + 4, :] = value[:, :4]
                out_ref[pl.ds(at, step), lo + 16 : lo + 20, :] = value[:, 4:]
        return carry

    lax.fori_loop(0, blocks // step, finish, 0)


def stay(array):
    return pltpu.with_memory_space_constraint(array, pltpu.HBM)


def patch_gradient(z, probe, spots, counts, tables, resident, group=GROUP):
    strips = z.shape[0]
    vmem = pl.BlockSpec(memory_space=pltpu.VMEM)
    hbm = pl.BlockSpec(memory_space=pltpu.HBM)
    inputs = (counts, probe, *tables)
    out = pl.pallas_call(
        functools.partial(patch_kernel, group),
        out_shape=jax.ShapeDtypeStruct((strips // 2, 32, LEN), jnp.float32),
        in_specs=[vmem, hbm] + [vmem if resident else hbm] * len(inputs),
        out_specs=vmem,
        scratch_shapes=[
            pltpu.VMEM((4, 4 * strips, LEN), jnp.float32),
            pltpu.VMEM((4, 4 * strips, LEN), jnp.float32),
            pltpu.SMEM(spots.shape, jnp.int32),
            *([] if resident else [pltpu.VMEM(x.shape, x.dtype) for x in inputs]),
            pltpu.SemaphoreType.DMA((5,)),
        ],
        compiler_params=pltpu.CompilerParams(vmem_limit_bytes=16 << 20),
    )(z.reshape(strips // 2, 32, LEN), stay(spots), *(inputs if resident else [stay(x) for x in inputs]))
    return out.reshape(z.shape)


def mixed(planes, spectra, out_ref):
    materials = len(planes) // 2

    def one(e, carry):
        re = jnp.zeros_like(planes[0])
        im = jnp.zeros_like(planes[0])
        for m in range(materials):
            cr = spectra[2 * m, e]
            ci = spectra[2 * m + 1, e]
            re = re + cr * planes[m] - ci * planes[materials + m]
            im = im + cr * planes[materials + m] + ci * planes[m]
        out_ref[e, 0:8, :] = re
        out_ref[e, 8:16, :] = im
        return carry

    lax.fori_loop(0, out_ref.shape[0], one, 0, unroll=8)


def mix_kernel(spectra_hbm, maps_hbm, out_ref, maps, rows_ref, spectra, sems):
    copies = [
        pltpu.make_async_copy(spectra_hbm, spectra, sems.at[0]),
        pltpu.make_async_copy(maps_hbm, maps, sems.at[1]),
    ]
    for copy in copies:
        copy.start()
    for copy in copies:
        copy.wait()
    for half in range(2):
        rows_ref[:, 4 * half : 4 * half + 4, :] = maps[:, :, half * LEN : (half + 1) * LEN]
    mixed([rows_ref[p] for p in range(rows_ref.shape[0])], spectra, out_ref)


def unmix_kernel(factor, place, spectra, grads_ref, rows_ref, out_ref, near_ref, far_ref):
    materials = rows_ref.shape[0] // 2

    def one(e, sums):
        gr = grads_ref[e, 0:8, :]
        gi = grads_ref[e, 8:16, :]
        reals, imags = [], []
        for m in range(materials):
            cr = spectra[2 * m, e]
            ci = spectra[2 * m + 1, e]
            reals.append(sums[m] + cr * gr + ci * gi)
            imags.append(sums[materials + m] + cr * gi - ci * gr)
        return tuple(reals + imags)

    even = place[1] % 2 == 0
    zero = jnp.zeros(rows_ref.shape[1:], jnp.float32)
    sums = lax.fori_loop(0, grads_ref.shape[0], one, (zero,) * (2 * materials), unroll=8)
    for p in range(2 * materials):
        value = rows_ref[p] - factor * sums[p]
        out_ref[p] = value
        near_ref[p] = jnp.where(even, value[4:], value[:4])
        far_ref[p] = jnp.where(even, value[:4], value[4:])


def smooth(place, last, mine_ref, near_ref, far_ref, field):
    planes = mine_ref.shape[0]
    even = place[0] % 2 == 0
    for j in range(3):
        lanes = slice(j * LEN, (j + 1) * LEN)
        near = near_ref[:, 4 * j : 4 * j + 4, :]
        far = far_ref[:, 4 * j : 4 * j + 4, :]
        field[:, 0:4, lanes] = jnp.where(even, far, near)
        field[:, 4:8, lanes] = mine_ref[:, 4 * j : 4 * j + 4, :]
        field[:, 8:12, lanes] = jnp.where(even, near, far)
        field[:, 12:16, lanes] = jnp.zeros((planes, 4, LEN), jnp.float32)
    shape = (16, 3 * LEN)
    row = lax.broadcasted_iota(jnp.int32, shape, 0)
    lane = lax.broadcasted_iota(jnp.int32, shape, 1)
    low_row = jnp.where(place[0] == 0, 4, 0)
    high_row = jnp.where(place[0] == last[0], 8, 16)
    low_edge = jnp.where(place[1] == last[1], 2 * LEN + LEN // 2, 0)
    high_edge = jnp.where(place[1] == 0, 2 * LEN + LEN // 2, 3 * LEN)
    inside = (row >= low_row) & (row < high_row)
    inside = inside & ((lane < 2 * LEN) | ((lane >= low_edge) & (lane < high_edge)))
    results = [None] * planes
    for m in range(planes // 2):
        pair = [jnp.where(inside, field[p], 0.0) for p in (m, planes // 2 + m)]
        for _ in range(TV_STEPS):
            down = [pltpu.roll(x, 15, 0) - x for x in pair]
            across = [pltpu.roll(x, 3 * LEN - 1, 1) - x for x in pair]
            square = down[0] * down[0] + across[0] * across[0] + down[1] * down[1] + across[1] * across[1]
            scale = lax.rsqrt(square + TV_EPS)
            fresh = []
            for x, d, c in zip(pair, down, across):
                d = d * scale
                c = c * scale
                moved = x + TV_STEP * (d - pltpu.roll(d, 1, 0) + c - pltpu.roll(c, 1, 1))
                fresh.append(jnp.where(inside, moved, 0.0))
            pair = fresh
        results[m], results[planes // 2 + m] = pair
    return results


def smooth_mix_kernel(last, place, spectra, mine_ref, near_ref, far_ref, rows_ref, out_ref, field):
    results = smooth(place, last, mine_ref, near_ref, far_ref, field)
    for p, value in enumerate(results):
        rows_ref[p, 0:4, :] = value[4:8, :LEN]
        rows_ref[p, 4:8, :] = value[4:8, LEN : 2 * LEN]
    mixed([rows_ref[p] for p in range(rows_ref.shape[0])], spectra, out_ref)


def smooth_kernel(last, place, mine_ref, near_ref, far_ref, out_ref, field):
    results = smooth(place, last, mine_ref, near_ref, far_ref, field)
    for p, value in enumerate(results):
        out_ref[p] = value[4:8, : 2 * LEN]


def on_chip(kernel, out_shape, scalars, arrays, scratch=()):
    vmem = pl.BlockSpec(memory_space=pltpu.VMEM)
    smem = pl.BlockSpec(memory_space=pltpu.SMEM)
    return pl.pallas_call(
        kernel,
        out_shape=out_shape,
        in_specs=[smem] * len(scalars) + [vmem] * len(arrays),
        out_specs=jax.tree.map(lambda _: vmem, out_shape),
        scratch_shapes=list(scratch),
        compiler_params=pltpu.CompilerParams(vmem_limit_bytes=8 << 20),
    )(*scalars, *arrays)


def swaps(axis):
    count = lax.axis_size(axis)
    near = [(i, i ^ 1) for i in range(count)]
    return near, [((i + 1) % count, (k + 1) % count) for i, k in near]


def with_edges(rows, to_near, to_far, even):
    near, far = swaps("tile")
    from_near = lax.ppermute(to_near, "tile", near)
    from_far = lax.ppermute(to_far, "tile", far)
    lane = lax.broadcasted_iota(jnp.int32, from_near.shape, 2)
    return jnp.concatenate([rows, jnp.where((lane < LEN // 2) == even, from_near, from_far)], 1)


def from_neighbours(strip):
    near, far = swaps("energy")
    return lax.ppermute(strip, "energy", near), lax.ppermute(strip, "energy", far)


def shards(material_maps, spectra, probes, offsets, measured):
    energies, materials, _ = spectra.shape
    planes = 2 * materials
    rows, columns = material_maps.shape[2:]
    assert rows == 4 and columns == 2 * LEN
    probe = probes[0]
    spots = offsets[0].T
    counts = measured[0, 0]
    tables = dft_blocks(*dft_tables(LEN))
    weights = spectra.transpose(1, 2, 0).reshape(2 * materials, energies)
    factor = DATA_STEP / math.sqrt(energies)
    place = jnp.stack([lax.axis_index("energy"), lax.axis_index("tile")]).astype(jnp.int32)
    last = (lax.axis_size("energy") - 1, lax.axis_size("tile") - 1)
    strip = jax.ShapeDtypeStruct((planes, 2 * rows, LEN), jnp.float32)
    part = jax.ShapeDtypeStruct((planes, rows, LEN), jnp.float32)
    spread = jax.ShapeDtypeStruct((energies, 4 * rows, LEN), jnp.float32)
    field = pltpu.VMEM((planes, 16, 3 * LEN), jnp.float32)
    even = place[1] % 2 == 0
    maps, place, even = lax.optimization_barrier((material_maps.reshape(planes, rows, columns), place, even))
    current = maps.reshape(planes, rows, 2, LEN).transpose(0, 2, 1, 3).reshape(planes, 2 * rows, LEN)
    hbm = pl.BlockSpec(memory_space=pltpu.HBM)
    mixes = pl.pallas_call(
        mix_kernel,
        out_shape=spread,
        in_specs=[hbm, hbm],
        out_specs=pl.BlockSpec(memory_space=pltpu.VMEM),
        scratch_shapes=[
            pltpu.VMEM(maps.shape, jnp.float32),
            pltpu.VMEM(strip.shape, jnp.float32),
            pltpu.SMEM(weights.shape, jnp.float32),
            pltpu.SemaphoreType.DMA((2,)),
        ],
        compiler_params=pltpu.CompilerParams(vmem_limit_bytes=8 << 20),
    )(stay(weights), stay(maps))
    for repeat in range(ITERS):
        tile = lax.all_to_all(mixes, "energy", split_axis=0, concat_axis=0, tiled=True)
        grads = patch_gradient(tile, probe, spots, counts, tables, repeat > 0)
        grads = lax.all_to_all(grads, "energy", split_axis=0, concat_axis=0, tiled=True)
        current, to_near, to_far = on_chip(
            functools.partial(unmix_kernel, factor), (strip, part, part), (place, weights), (grads, current)
        )
        mine = with_edges(current, to_near, to_far, even)
        near, far = from_neighbours(mine)
        if repeat < ITERS - 1:
            current, mixes = on_chip(
                functools.partial(smooth_mix_kernel, last), (strip, spread), (place, weights), (mine, near, far), [field]
            )
    result = jax.ShapeDtypeStruct((planes, rows, columns), jnp.float32)
    out = on_chip(functools.partial(smooth_kernel, last), result, (place,), (mine, near, far), [field])
    return out.reshape(material_maps.shape)


def solution(mesh):
    in_specs = (
        P(None, None, "energy", "tile"),
        P(),
        P("energy", None, None),
        P("tile", None, None),
        P("energy", "tile", None, None, None),
    )
    out_specs = P(None, None, "energy", "tile")
    return jax.shard_map(shards, mesh=mesh, in_specs=in_specs, out_specs=out_specs, check_vma=False)
```

```python
import functools
import math

import jax
import jax.numpy as jnp
import numpy as np
from jax import lax
from jax.experimental import pallas as pl
from jax.experimental.pallas import tpu as pltpu
from jax.sharding import PartitionSpec as P

ITERS = 2
TV_STEPS = 3
DATA_STEP = 0.05
TV_STEP = 0.05
TV_EPS = 0.01

LEN = 128
GROUP = 16
LIMIT = 4096.0

def dft_tables(length):
    index = np.arange(length)
    angle = (index[:, None] * index[None, :] % length) * (-2.0 * math.pi / length)
    scale = 1.0 / math.sqrt(length)
    return tuple((wave(angle) * scale).astype(np.float32).astype(jnp.bfloat16) for wave in (np.cos, np.sin))


def dft_blocks(fr, fi):
    ahead = np.block([[fr, fi], [-fi, fr]])
    back = np.block([[fr, -fi], [fi, fr]])
    return jnp.asarray(ahead), jnp.asarray(back)


def dot(left, right):
    return jnp.dot(left, right, preferred_element_type=jnp.float32)

def pair_up(both):
    one, two = both
    return jnp.concatenate([
        jnp.concatenate([one[:, :LEN], two[:, :LEN]], 1),
        jnp.concatenate([one[:, LEN:], two[:, LEN:]], 1)], 0)

def sine_cosine(angle):
    turns = jnp.floor(angle * (2.0 / math.pi) + 0.5)
    rest = ((angle - turns * 1.5703125) - turns * 4.837512969970703125e-4) - turns * 7.54978995489188216e-8
    quadrant = turns.astype(jnp.int32)
    square = rest * rest
    sine = ((-1.9515295891e-4 * square + 8.3321608736e-3) * square - 1.6666654611e-1) * square * rest + rest
    cosine = ((2.443315711809948e-5 * square - 1.388731625493765e-3) * square + 4.166664568298827e-2) * square * square
    cosine = cosine - 0.5 * square + 1.0
    odd = (quadrant & 1) == 1
    first = jnp.where(odd, cosine, sine)
    second = jnp.where(odd, sine, cosine)
    return (
        jnp.where((quadrant & 2) == 2, -first, first),
        jnp.where(((quadrant + 1) & 2) == 2, -second, second),
    )


def patch_kernel(
    group, z_ref, spots_hbm, counts, probe_ref, ahead_ref, back_ref, out_ref, wave, total, spots, sem
):
    copy = pltpu.make_async_copy(spots_hbm, spots, sem)
    copy.start()
    patches = counts.shape[0]
    blocks = z_ref.shape[0]
    step = 4
    upper = lax.broadcasted_iota(jnp.int32, (step, 8, LEN), 1) < 4

    def parts(i, half):
        at = pl.multiple_of(i * step, step)
        rows = pl.ds(pl.multiple_of(i * step * 8, step * 8), step * 8)

        def part(c):
            low = z_ref[pl.ds(at, step), 8 * c + 4 * half : 8 * c + 4 * half + 8, :]
            high = z_ref[pl.ds(at, step), 8 * c + 4 * half + 12 : 8 * c + 4 * half + 20, :]
            return jnp.where(upper, low, high).reshape(step * 8, LEN)

        return rows, part(0), part(1)

    def expand(i, largest):
        for half in range(2):
            rows, size, angle = parts(i, half)
            growth = jnp.exp(size)
            sine, cosine = sine_cosine(angle)
            wave[half, rows, :] = growth * cosine
            wave[2 + half, rows, :] = growth * sine
            total[half, rows, :] = jnp.zeros((step * 8, LEN), jnp.float32)
            total[2 + half, rows, :] = jnp.zeros((step * 8, LEN), jnp.float32)
            largest = jnp.maximum(largest, jnp.abs(angle))
        return largest

    largest = lax.fori_loop(0, blocks // step, expand, jnp.zeros((step * 8, LEN), jnp.float32))

    @pl.when(jnp.max(largest) > LIMIT)
    def _():
        def again(i, carry):
            for half in range(2):
                rows, size, angle = parts(i, half)
                growth = jnp.exp(size)
                wave[half, rows, :] = growth * jnp.cos(angle)
                wave[2 + half, rows, :] = growth * jnp.sin(angle)
            return carry

        lax.fori_loop(0, blocks // step, again, 0)

    copy.wait()
    lane = lax.broadcasted_iota(jnp.int32, (LEN, LEN), 1)

    def one_group(g, carry):
        first = g * group
        exits = []
        for j in range(group):
            a = spots[0, first + j]
            b = spots[1, first + j]
            rows = pl.ds(a, LEN)
            keep = lane >= b
            shift = jnp.bitwise_and(LEN - b, LEN - 1)
            wr = pltpu.roll(jnp.where(keep, wave[0, rows, :], wave[1, rows, :]), shift, 1)
            wi = pltpu.roll(jnp.where(keep, wave[2, rows, :], wave[3, rows, :]), shift, 1)
            pr = probe_ref[:, :LEN]
            pi = probe_ref[:, LEN:]
            exits.append(jnp.concatenate([pr * wr - pi * wi, pr * wi + pi * wr], 1).astype(jnp.bfloat16))
        first_pass = dot(jnp.concatenate(exits, 0), ahead_ref[...]).astype(jnp.bfloat16)
        weighted = []
        for j in range(0, group, 2):
            far = dot(back_ref[...], pair_up([first_pass[k * LEN : (k + 1) * LEN] for k in (j, j + 1)]))
            for k in range(2):
                fr = far[:LEN, k * LEN : (k + 1) * LEN]
                fi = far[LEN:, k * LEN : (k + 1) * LEN]
                misfit = fr * fr + fi * fi - counts[first + j + k]
                weighted.append(jnp.concatenate([misfit * fr, misfit * fi], 1).astype(jnp.bfloat16))
        third_pass = dot(jnp.concatenate(weighted, 0), back_ref[...]).astype(jnp.bfloat16)
        for j in range(0, group, 2):
            grad = dot(ahead_ref[...], pair_up([third_pass[k * LEN : (k + 1) * LEN] for k in (j, j + 1)]))
            for k in range(2):
                a = spots[0, first + j + k]
                b = spots[1, first + j + k]
                rows = pl.ds(a, LEN)
                gr = grad[:LEN, k * LEN : (k + 1) * LEN]
                gi = grad[LEN:, k * LEN : (k + 1) * LEN]
                pr = probe_ref[:, :LEN]
                pi = probe_ref[:, LEN:]
                keep = lane >= b
                shift = jnp.bitwise_and(b, LEN - 1)
                ur = pltpu.roll(pr * gr + pi * gi, shift, 1)
                ui = pltpu.roll(pr * gi - pi * gr, shift, 1)
                total[0, rows, :] += jnp.where(keep, ur, 0.0)
                total[1, rows, :] += jnp.where(keep, 0.0, ur)
                total[2, rows, :] += jnp.where(keep, ui, 0.0)
                total[3, rows, :] += jnp.where(keep, 0.0, ui)
        return carry

    lax.fori_loop(0, patches // group, one_group, 0)

    def finish(i, carry):
        at = pl.multiple_of(i * step, step)
        rows = pl.ds(pl.multiple_of(i * step * 8, step * 8), step * 8)
        for half in range(2):
            orr = wave[half, rows, :]
            oi = wave[2 + half, rows, :]
            tr = total[half, rows, :]
            ti = total[2 + half, rows, :]
            for c, value in ((0, orr * tr + oi * ti), (1, orr * ti - oi * tr)):
                value = value.reshape(step, 8, LEN)
                lo = 8 * c + 4 * half
                out_ref[pl.ds(at, step), lo : lo + 4, :] = value[:, :4]
                out_ref[pl.ds(at, step), lo + 16 : lo + 20, :] = value[:, 4:]
        return carry

    lax.fori_loop(0, blocks // step, finish, 0)


def stay(array):
    return pltpu.with_memory_space_constraint(array, pltpu.HBM)


def patch_gradient(z, probe, spots, counts, tables, group=GROUP):
    strips = z.shape[0]
    vmem = pl.BlockSpec(memory_space=pltpu.VMEM)
    hbm = pl.BlockSpec(memory_space=pltpu.HBM)
    inputs = (counts, probe, *tables)
    out = pl.pallas_call(
        functools.partial(patch_kernel, group),
        out_shape=jax.ShapeDtypeStruct((strips // 2, 32, LEN), jnp.float32),
        in_specs=[vmem, hbm] + [vmem] * len(inputs),
        out_specs=vmem,
        scratch_shapes=[
            pltpu.VMEM((4, 4 * strips, LEN), jnp.float32),
            pltpu.VMEM((4, 4 * strips, LEN), jnp.float32),
            pltpu.SMEM(spots.shape, jnp.int32),
            pltpu.SemaphoreType.DMA,
        ],
        compiler_params=pltpu.CompilerParams(vmem_limit_bytes=16 << 20),
    )(z.reshape(strips // 2, 32, LEN), stay(spots), *inputs)
    return out.reshape(z.shape)


def mixed(planes, spectra, out_ref):
    materials = len(planes) // 2

    def one(e, carry):
        re = jnp.zeros_like(planes[0])
        im = jnp.zeros_like(planes[0])
        for m in range(materials):
            cr = spectra[2 * m, e]
            ci = spectra[2 * m + 1, e]
            re = re + cr * planes[m] - ci * planes[materials + m]
            im = im + cr * planes[materials + m] + ci * planes[m]
        out_ref[e, 0:8, :] = re
        out_ref[e, 8:16, :] = im
        return carry

    lax.fori_loop(0, out_ref.shape[0], one, 0, unroll=8)


def mix_kernel(spectra_hbm, maps_hbm, *rest):
    out_ref, maps, rows_ref, spectra, sems = rest[-5:]
    copies = [
        pltpu.make_async_copy(spectra_hbm, spectra, sems.at[0]),
        pltpu.make_async_copy(maps_hbm, maps, sems.at[1]),
    ]
    for copy in copies:
        copy.start()
    for copy in copies:
        copy.wait()
    for half in range(2):
        rows_ref[:, 4 * half : 4 * half + 4, :] = maps[:, :, half * LEN : (half + 1) * LEN]
    mixed([rows_ref[p] for p in range(rows_ref.shape[0])], spectra, out_ref)


def unmix_kernel(factor, place, spectra, grads_ref, rows_ref, out_ref, near_ref, far_ref):
    materials = rows_ref.shape[0] // 2

    def one(e, sums):
        gr = grads_ref[e, 0:8, :]
        gi = grads_ref[e, 8:16, :]
        reals, imags = [], []
        for m in range(materials):
            cr = spectra[2 * m, e]
            ci = spectra[2 * m + 1, e]
            reals.append(sums[m] + cr * gr + ci * gi)
            imags.append(sums[materials + m] + cr * gi - ci * gr)
        return tuple(reals + imags)

    even = place[1] % 2 == 0
    zero = jnp.zeros(rows_ref.shape[1:], jnp.float32)
    sums = lax.fori_loop(0, grads_ref.shape[0], one, (zero,) * (2 * materials), unroll=8)
    for p in range(2 * materials):
        value = rows_ref[p] - factor * sums[p]
        out_ref[p] = value
        near_ref[p] = jnp.where(even, value[4:], value[:4])
        far_ref[p] = jnp.where(even, value[:4], value[4:])


def smooth(place, last, mine_ref, near_ref, far_ref, field):
    planes = mine_ref.shape[0]
    even = place[0] % 2 == 0
    for j in range(3):
        lanes = slice(j * LEN, (j + 1) * LEN)
        near = near_ref[:, 4 * j : 4 * j + 4, :]
        far = far_ref[:, 4 * j : 4 * j + 4, :]
        field[:, 0:4, lanes] = jnp.where(even, far, near)
        field[:, 4:8, lanes] = mine_ref[:, 4 * j : 4 * j + 4, :]
        field[:, 8:12, lanes] = jnp.where(even, near, far)
        field[:, 12:16, lanes] = jnp.zeros((planes, 4, LEN), jnp.float32)
    shape = (16, 3 * LEN)
    row = lax.broadcasted_iota(jnp.int32, shape, 0)
    lane = lax.broadcasted_iota(jnp.int32, shape, 1)
    low_row = jnp.where(place[0] == 0, 4, 0)
    high_row = jnp.where(place[0] == last[0], 8, 16)
    low_edge = jnp.where(place[1] == last[1], 2 * LEN + LEN // 2, 0)
    high_edge = jnp.where(place[1] == 0, 2 * LEN + LEN // 2, 3 * LEN)
    inside = (row >= low_row) & (row < high_row)
    inside = inside & ((lane < 2 * LEN) | ((lane >= low_edge) & (lane < high_edge)))
    results = [None] * planes
    for m in range(planes // 2):
        pair = [jnp.where(inside, field[p], 0.0) for p in (m, planes // 2 + m)]
        for _ in range(TV_STEPS):
            down = [pltpu.roll(x, 15, 0) - x for x in pair]
            across = [pltpu.roll(x, 3 * LEN - 1, 1) - x for x in pair]
            square = down[0] * down[0] + across[0] * across[0] + down[1] * down[1] + across[1] * across[1]
            scale = lax.rsqrt(square + TV_EPS)
            fresh = []
            for x, d, c in zip(pair, down, across):
                d = d * scale
                c = c * scale
                moved = x + TV_STEP * (d - pltpu.roll(d, 1, 0) + c - pltpu.roll(c, 1, 1))
                fresh.append(jnp.where(inside, moved, 0.0))
            pair = fresh
        results[m], results[planes // 2 + m] = pair
    return results


def smooth_mix_kernel(last, place, spectra, mine_ref, near_ref, far_ref, rows_ref, out_ref, field):
    results = smooth(place, last, mine_ref, near_ref, far_ref, field)
    for p, value in enumerate(results):
        rows_ref[p, 0:4, :] = value[4:8, :LEN]
        rows_ref[p, 4:8, :] = value[4:8, LEN : 2 * LEN]
    mixed([rows_ref[p] for p in range(rows_ref.shape[0])], spectra, out_ref)


def smooth_kernel(last, place, mine_ref, near_ref, far_ref, out_ref, field):
    results = smooth(place, last, mine_ref, near_ref, far_ref, field)
    for p, value in enumerate(results):
        out_ref[p] = value[4:8, : 2 * LEN]


def on_chip(kernel, out_shape, scalars, arrays, scratch=()):
    vmem = pl.BlockSpec(memory_space=pltpu.VMEM)
    smem = pl.BlockSpec(memory_space=pltpu.SMEM)
    return pl.pallas_call(
        kernel,
        out_shape=out_shape,
        in_specs=[smem] * len(scalars) + [vmem] * len(arrays),
        out_specs=jax.tree.map(lambda _: vmem, out_shape),
        scratch_shapes=list(scratch),
        compiler_params=pltpu.CompilerParams(vmem_limit_bytes=8 << 20),
    )(*scalars, *arrays)


def swaps(axis):
    count = lax.axis_size(axis)
    near = [(i, i ^ 1) for i in range(count)]
    return near, [((i + 1) % count, (k + 1) % count) for i, k in near]


def with_edges(rows, to_near, to_far, even):
    near, far = swaps("tile")
    from_near = lax.ppermute(to_near, "tile", near)
    from_far = lax.ppermute(to_far, "tile", far)
    lane = lax.broadcasted_iota(jnp.int32, from_near.shape, 2)
    return jnp.concatenate([rows, jnp.where((lane < LEN // 2) == even, from_near, from_far)], 1)


def from_neighbours(strip):
    near, far = swaps("energy")
    return lax.ppermute(strip, "energy", near), lax.ppermute(strip, "energy", far)


def shards(material_maps, spectra, probes, offsets, measured):
    energies, materials, _ = spectra.shape
    planes = 2 * materials
    rows, columns = material_maps.shape[2:]
    assert rows == 4 and columns == 2 * LEN
    probe = probes[0]
    spots = offsets[0].T
    counts = measured[0, 0]
    tables = dft_blocks(*dft_tables(LEN))
    weights = spectra.transpose(1, 2, 0).reshape(2 * materials, energies)
    factor = DATA_STEP / math.sqrt(energies)
    place = jnp.stack([lax.axis_index("energy"), lax.axis_index("tile")]).astype(jnp.int32)
    last = (lax.axis_size("energy") - 1, lax.axis_size("tile") - 1)
    strip = jax.ShapeDtypeStruct((planes, 2 * rows, LEN), jnp.float32)
    part = jax.ShapeDtypeStruct((planes, rows, LEN), jnp.float32)
    spread = jax.ShapeDtypeStruct((energies, 4 * rows, LEN), jnp.float32)
    field = pltpu.VMEM((planes, 16, 3 * LEN), jnp.float32)
    even = place[1] % 2 == 0
    maps, place, even = lax.optimization_barrier((material_maps.reshape(planes, rows, columns), place, even))
    current = maps.reshape(planes, rows, 2, LEN).transpose(0, 2, 1, 3).reshape(planes, 2 * rows, LEN)
    hbm = pl.BlockSpec(memory_space=pltpu.HBM)
    later = (counts, probe, *tables)
    mixes = pl.pallas_call(
        mix_kernel,
        out_shape=spread,
        in_specs=[hbm] * (2 + len(later)),
        out_specs=pl.BlockSpec(memory_space=pltpu.VMEM),
        scratch_shapes=[
            pltpu.VMEM(maps.shape, jnp.float32),
            pltpu.VMEM(strip.shape, jnp.float32),
            pltpu.SMEM(weights.shape, jnp.float32),
            pltpu.SemaphoreType.DMA((2,)),
        ],
        compiler_params=pltpu.CompilerParams(vmem_limit_bytes=8 << 20),
    )(*[stay(x) for x in (weights, maps, *later)])
    for repeat in range(ITERS):
        tile = lax.all_to_all(mixes, "energy", split_axis=0, concat_axis=0, tiled=True)
        grads = patch_gradient(tile, probe, spots, counts, tables)
        grads = lax.all_to_all(grads, "energy", split_axis=0, concat_axis=0, tiled=True)
        current, to_near, to_far = on_chip(
            functools.partial(unmix_kernel, factor), (strip, part, part), (place, weights), (grads, current)
        )
        mine = with_edges(current, to_near, to_far, even)
        near, far = from_neighbours(mine)
        if repeat < ITERS - 1:
            current, mixes = on_chip(
                functools.partial(smooth_mix_kernel, last), (strip, spread), (place, weights), (mine, near, far), [field]
            )
    result = jax.ShapeDtypeStruct((planes, rows, columns), jnp.float32)
    out = on_chip(functools.partial(smooth_kernel, last), result, (place,), (mine, near, far), [field])
    return out.reshape(material_maps.shape)


def solution(mesh):
    in_specs = (
        P(None, None, "energy", "tile"),
        P(),
        P("energy", None, None),
        P("tile", None, None),
        P("energy", "tile", None, None, None),
    )
    out_specs = P(None, None, "energy", "tile")
    return jax.shard_map(shards, mesh=mesh, in_specs=in_specs, out_specs=out_specs, check_vma=False)
```

```python
import functools
import math

import jax
import jax.numpy as jnp
import numpy as np
from jax import lax
from jax.experimental import pallas as pl
from jax.experimental.pallas import tpu as pltpu
from jax.sharding import PartitionSpec as P

ITERS = 2
TV_STEPS = 3
DATA_STEP = 0.05
TV_STEP = 0.05
TV_EPS = 0.01

LEN = 128
GROUP = 16
LIMIT = 4096.0

def dft_tables(length):
    index = np.arange(length)
    angle = (index[:, None] * index[None, :] % length) * (-2.0 * math.pi / length)
    scale = 1.0 / math.sqrt(length)
    return tuple((wave(angle) * scale).astype(np.float32).astype(jnp.bfloat16) for wave in (np.cos, np.sin))


def dft_blocks(fr, fi):
    ahead = np.block([[fr, fi], [-fi, fr]])
    back = np.block([[fr, -fi], [fi, fr]])
    return jnp.asarray(ahead), jnp.asarray(back)


def dot(left, right):
    return jnp.dot(left, right, preferred_element_type=jnp.float32)

def pair_up(both):
    one, two = both
    return jnp.concatenate([
        jnp.concatenate([one[:, :LEN], two[:, :LEN]], 1),
        jnp.concatenate([one[:, LEN:], two[:, LEN:]], 1)], 0)

def sine_cosine(angle):
    turns = jnp.floor(angle * (2.0 / math.pi) + 0.5)
    rest = ((angle - turns * 1.5703125) - turns * 4.837512969970703125e-4) - turns * 7.54978995489188216e-8
    quadrant = turns.astype(jnp.int32)
    square = rest * rest
    sine = ((-1.9515295891e-4 * square + 8.3321608736e-3) * square - 1.6666654611e-1) * square * rest + rest
    cosine = ((2.443315711809948e-5 * square - 1.388731625493765e-3) * square + 4.166664568298827e-2) * square * square
    cosine = cosine - 0.5 * square + 1.0
    odd = (quadrant & 1) == 1
    first = jnp.where(odd, cosine, sine)
    second = jnp.where(odd, sine, cosine)
    return (
        jnp.where((quadrant & 2) == 2, -first, first),
        jnp.where(((quadrant + 1) & 2) == 2, -second, second),
    )


def patch_kernel(
    group, z_ref, spots_hbm, counts, probe_ref, ahead_ref, back_ref, out_ref, wave, total, spots, sem
):
    copy = pltpu.make_async_copy(spots_hbm, spots, sem)
    copy.start()
    patches = counts.shape[0]
    blocks = z_ref.shape[0]
    step = 4
    upper = lax.broadcasted_iota(jnp.int32, (step, 8, LEN), 1) < 4

    def parts(i, half):
        at = pl.multiple_of(i * step, step)
        rows = pl.ds(pl.multiple_of(i * step * 8, step * 8), step * 8)

        def part(c):
            low = z_ref[pl.ds(at, step), 8 * c + 4 * half : 8 * c + 4 * half + 8, :]
            high = z_ref[pl.ds(at, step), 8 * c + 4 * half + 12 : 8 * c + 4 * half + 20, :]
            return jnp.where(upper, low, high).reshape(step * 8, LEN)

        return rows, part(0), part(1)

    def expand(i, largest):
        for half in range(2):
            rows, size, angle = parts(i, half)
            growth = jnp.exp(size)
            sine, cosine = sine_cosine(angle)
            wave[half, rows, :] = growth * cosine
            wave[2 + half, rows, :] = growth * sine
            total[half, rows, :] = jnp.zeros((step * 8, LEN), jnp.float32)
            total[2 + half, rows, :] = jnp.zeros((step * 8, LEN), jnp.float32)
            largest = jnp.maximum(largest, jnp.abs(angle))
        return largest

    largest = lax.fori_loop(0, blocks // step, expand, jnp.zeros((step * 8, LEN), jnp.float32))

    @pl.when(jnp.max(largest) > LIMIT)
    def _():
        def again(i, carry):
            for half in range(2):
                rows, size, angle = parts(i, half)
                growth = jnp.exp(size)
                wave[half, rows, :] = growth * jnp.cos(angle)
                wave[2 + half, rows, :] = growth * jnp.sin(angle)
            return carry

        lax.fori_loop(0, blocks // step, again, 0)

    copy.wait()
    lane = lax.broadcasted_iota(jnp.int32, (LEN, LEN), 1)

    def one_group(g, carry):
        first = g * group
        exits = []
        for j in range(group):
            a = spots[0, first + j]
            b = spots[1, first + j]
            rows = pl.ds(a, LEN)
            keep = lane >= b
            shift = jnp.bitwise_and(LEN - b, LEN - 1)
            wr = pltpu.roll(jnp.where(keep, wave[0, rows, :], wave[1, rows, :]), shift, 1)
            wi = pltpu.roll(jnp.where(keep, wave[2, rows, :], wave[3, rows, :]), shift, 1)
            pr = probe_ref[:, :LEN]
            pi = probe_ref[:, LEN:]
            exits.append(jnp.concatenate([pr * wr - pi * wi, pr * wi + pi * wr], 1).astype(jnp.bfloat16))
        first_pass = dot(jnp.concatenate(exits, 0), ahead_ref[...]).astype(jnp.bfloat16)
        weighted = []
        for j in range(0, group, 2):
            far = dot(back_ref[...], pair_up([first_pass[k * LEN : (k + 1) * LEN] for k in (j, j + 1)]))
            for k in range(2):
                fr = far[:LEN, k * LEN : (k + 1) * LEN]
                fi = far[LEN:, k * LEN : (k + 1) * LEN]
                misfit = fr * fr + fi * fi - counts[first + j + k]
                weighted.append(jnp.concatenate([misfit * fr, misfit * fi], 1).astype(jnp.bfloat16))
        third_pass = dot(jnp.concatenate(weighted, 0), back_ref[...]).astype(jnp.bfloat16)
        for j in range(0, group, 2):
            grad = dot(ahead_ref[...], pair_up([third_pass[k * LEN : (k + 1) * LEN] for k in (j, j + 1)]))
            for k in range(2):
                a = spots[0, first + j + k]
                b = spots[1, first + j + k]
                rows = pl.ds(a, LEN)
                gr = grad[:LEN, k * LEN : (k + 1) * LEN]
                gi = grad[LEN:, k * LEN : (k + 1) * LEN]
                pr = probe_ref[:, :LEN]
                pi = probe_ref[:, LEN:]
                keep = lane >= b
                shift = jnp.bitwise_and(b, LEN - 1)
                ur = pltpu.roll(pr * gr + pi * gi, shift, 1)
                ui = pltpu.roll(pr * gi - pi * gr, shift, 1)
                total[0, rows, :] += jnp.where(keep, ur, 0.0)
                total[1, rows, :] += jnp.where(keep, 0.0, ur)
                total[2, rows, :] += jnp.where(keep, ui, 0.0)
                total[3, rows, :] += jnp.where(keep, 0.0, ui)
        return carry

    lax.fori_loop(0, patches // group, one_group, 0)

    def finish(i, carry):
        at = pl.multiple_of(i * step, step)
        rows = pl.ds(pl.multiple_of(i * step * 8, step * 8), step * 8)
        for half in range(2):
            orr = wave[half, rows, :]
            oi = wave[2 + half, rows, :]
            tr = total[half, rows, :]
            ti = total[2 + half, rows, :]
            for c, value in ((0, orr * tr + oi * ti), (1, orr * ti - oi * tr)):
                value = value.reshape(step, 8, LEN)
                lo = 8 * c + 4 * half
                out_ref[pl.ds(at, step), lo : lo + 4, :] = value[:, :4]
                out_ref[pl.ds(at, step), lo + 16 : lo + 20, :] = value[:, 4:]
        return carry

    lax.fori_loop(0, blocks // step, finish, 0)


def stay(array):
    return pltpu.with_memory_space_constraint(array, pltpu.HBM)


def patch_gradient(z, probe, spots, counts, tables, group=GROUP):
    strips = z.shape[0]
    vmem = pl.BlockSpec(memory_space=pltpu.VMEM)
    hbm = pl.BlockSpec(memory_space=pltpu.HBM)
    inputs = (counts, probe, *tables)
    out = pl.pallas_call(
        functools.partial(patch_kernel, group),
        out_shape=jax.ShapeDtypeStruct((strips // 2, 32, LEN), jnp.float32),
        in_specs=[vmem, hbm] + [vmem] * len(inputs),
        out_specs=vmem,
        scratch_shapes=[
            pltpu.VMEM((4, 4 * strips, LEN), jnp.float32),
            pltpu.VMEM((4, 4 * strips, LEN), jnp.float32),
            pltpu.SMEM(spots.shape, jnp.int32),
            pltpu.SemaphoreType.DMA,
        ],
        compiler_params=pltpu.CompilerParams(vmem_limit_bytes=16 << 20),
    )(z.reshape(strips // 2, 32, LEN), stay(spots), *inputs)
    return out.reshape(z.shape)


def mixed(planes, spectra, out_ref):
    materials = len(planes) // 2

    def one(e, carry):
        re = jnp.zeros_like(planes[0])
        im = jnp.zeros_like(planes[0])
        for m in range(materials):
            cr = spectra[2 * m, e]
            ci = spectra[2 * m + 1, e]
            re = re + cr * planes[m] - ci * planes[materials + m]
            im = im + cr * planes[materials + m] + ci * planes[m]
        out_ref[e, 0:8, :] = re
        out_ref[e, 8:16, :] = im
        return carry

    lax.fori_loop(0, out_ref.shape[0], one, 0, unroll=8)


def mix_kernel(spectra_hbm, maps_hbm, *rest):
    out_ref, maps, rows_ref, spectra, sems = rest[-5:]
    copies = [
        pltpu.make_async_copy(spectra_hbm, spectra, sems.at[0]),
        pltpu.make_async_copy(maps_hbm, maps, sems.at[1]),
    ]
    for copy in copies:
        copy.start()
    for copy in copies:
        copy.wait()
    for half in range(2):
        rows_ref[:, 4 * half : 4 * half + 4, :] = maps[:, :, half * LEN : (half + 1) * LEN]
    mixed([rows_ref[p] for p in range(rows_ref.shape[0])], spectra, out_ref)


def unmix_kernel(factor, place, spectra, grads_ref, rows_ref, out_ref, far_ref, near_ref):
    materials = rows_ref.shape[0] // 2

    def one(e, sums):
        gr = grads_ref[e, 0:8, :]
        gi = grads_ref[e, 8:16, :]
        reals, imags = [], []
        for m in range(materials):
            cr = spectra[2 * m, e]
            ci = spectra[2 * m + 1, e]
            reals.append(sums[m] + cr * gr + ci * gi)
            imags.append(sums[materials + m] + cr * gi - ci * gr)
        return tuple(reals + imags)

    even = place[1] % 2 == 0
    zero = jnp.zeros(rows_ref.shape[1:], jnp.float32)
    sums = lax.fori_loop(0, grads_ref.shape[0], one, (zero,) * (2 * materials), unroll=8)
    for p in range(2 * materials):
        value = rows_ref[p] - factor * sums[p]
        out_ref[p] = value
        near_ref[p] = jnp.where(even, value[4:], value[:4])
        far_ref[p] = jnp.where(even, value[:4], value[4:])


def smooth(place, last, mine_ref, near_ref, far_ref, field):
    planes = field.shape[0]
    even = place[0] % 2 == 0
    for p in range(planes):
        for j in range(3):
            rows = slice(8 * p + 4 * j, 8 * p + 4 * j + 4) if j < 2 else slice(8 * planes + 4 * p, 8 * planes + 4 * p + 4)
            lanes = slice(j * LEN, (j + 1) * LEN)
            near = near_ref[rows, :]
            far = far_ref[rows, :]
            field[p, 0:4, lanes] = jnp.where(even, far, near)
            field[p, 4:8, lanes] = mine_ref[rows, :]
            field[p, 8:12, lanes] = jnp.where(even, near, far)
            field[p, 12:16, lanes] = jnp.zeros((4, LEN), jnp.float32)
    shape = (16, 3 * LEN)
    row = lax.broadcasted_iota(jnp.int32, shape, 0)
    lane = lax.broadcasted_iota(jnp.int32, shape, 1)
    low_row = jnp.where(place[0] == 0, 4, 0)
    high_row = jnp.where(place[0] == last[0], 8, 16)
    low_edge = jnp.where(place[1] == last[1], 2 * LEN + LEN // 2, 0)
    high_edge = jnp.where(place[1] == 0, 2 * LEN + LEN // 2, 3 * LEN)
    inside = (row >= low_row) & (row < high_row)
    inside = inside & ((lane < 2 * LEN) | ((lane >= low_edge) & (lane < high_edge)))
    results = [None] * planes
    for m in range(planes // 2):
        pair = [jnp.where(inside, field[p], 0.0) for p in (m, planes // 2 + m)]
        for _ in range(TV_STEPS):
            down = [pltpu.roll(x, 15, 0) - x for x in pair]
            across = [pltpu.roll(x, 3 * LEN - 1, 1) - x for x in pair]
            square = down[0] * down[0] + across[0] * across[0] + down[1] * down[1] + across[1] * across[1]
            scale = lax.rsqrt(square + TV_EPS)
            fresh = []
            for x, d, c in zip(pair, down, across):
                d = d * scale
                c = c * scale
                moved = x + TV_STEP * (d - pltpu.roll(d, 1, 0) + c - pltpu.roll(c, 1, 1))
                fresh.append(jnp.where(inside, moved, 0.0))
            pair = fresh
        results[m], results[planes // 2 + m] = pair
    return results


def smooth_mix_kernel(last, place, spectra, mine_ref, near_ref, far_ref, rows_ref, out_ref, field):
    results = smooth(place, last, mine_ref, near_ref, far_ref, field)
    for p, value in enumerate(results):
        rows_ref[p, 0:4, :] = value[4:8, :LEN]
        rows_ref[p, 4:8, :] = value[4:8, LEN : 2 * LEN]
    mixed([rows_ref[p] for p in range(rows_ref.shape[0])], spectra, out_ref)


def smooth_kernel(last, place, mine_ref, near_ref, far_ref, out_ref, field):
    results = smooth(place, last, mine_ref, near_ref, far_ref, field)
    for p, value in enumerate(results):
        out_ref[p] = value[4:8, : 2 * LEN]


def on_chip(kernel, out_shape, scalars, arrays, scratch=()):
    vmem = pl.BlockSpec(memory_space=pltpu.VMEM)
    smem = pl.BlockSpec(memory_space=pltpu.SMEM)
    return pl.pallas_call(
        kernel,
        out_shape=out_shape,
        in_specs=[smem] * len(scalars) + [vmem] * len(arrays),
        out_specs=jax.tree.map(lambda _: vmem, out_shape),
        scratch_shapes=list(scratch),
        compiler_params=pltpu.CompilerParams(vmem_limit_bytes=8 << 20),
    )(*scalars, *arrays)


def swaps(axis):
    count = lax.axis_size(axis)
    near = [(i, i ^ 1) for i in range(count)]
    return near, [((i + 1) % count, (k + 1) % count) for i, k in near]


def with_edges(rows, to_near, to_far, even):
    near, far = swaps("tile")
    from_far = lax.ppermute(to_far, "tile", far)
    from_near = lax.ppermute(to_near, "tile", near)
    lane = lax.broadcasted_iota(jnp.int32, from_near.shape, 2)
    edges = jnp.where((lane < LEN // 2) != even, from_far, from_near)
    return jnp.concatenate([rows.reshape(-1, LEN), edges.reshape(-1, LEN)], 0)


def from_neighbours(strip):
    near, far = swaps("energy")
    return lax.ppermute(strip, "energy", near), lax.ppermute(strip, "energy", far)


def shards(material_maps, spectra, probes, offsets, measured):
    energies, materials, _ = spectra.shape
    planes = 2 * materials
    rows, columns = material_maps.shape[2:]
    assert rows == 4 and columns == 2 * LEN
    probe = probes[0]
    spots = offsets[0].T
    counts = measured[0, 0]
    tables = dft_blocks(*dft_tables(LEN))
    weights = spectra.transpose(1, 2, 0).reshape(2 * materials, energies)
    factor = DATA_STEP / math.sqrt(energies)
    place = jnp.stack([lax.axis_index("energy"), lax.axis_index("tile")]).astype(jnp.int32)
    last = (lax.axis_size("energy") - 1, lax.axis_size("tile") - 1)
    strip = jax.ShapeDtypeStruct((planes, 2 * rows, LEN), jnp.float32)
    part = jax.ShapeDtypeStruct((planes, rows, LEN), jnp.float32)
    spread = jax.ShapeDtypeStruct((energies, 4 * rows, LEN), jnp.float32)
    field = pltpu.VMEM((planes, 16, 3 * LEN), jnp.float32)
    even = place[1] % 2 == 0
    maps, place, even = lax.optimization_barrier((material_maps.reshape(planes, rows, columns), place, even))
    current = maps.reshape(planes, rows, 2, LEN).transpose(0, 2, 1, 3).reshape(planes, 2 * rows, LEN)
    hbm = pl.BlockSpec(memory_space=pltpu.HBM)
    later = (counts, probe, *tables)
    mixes = pl.pallas_call(
        mix_kernel,
        out_shape=spread,
        in_specs=[hbm] * (2 + len(later)),
        out_specs=pl.BlockSpec(memory_space=pltpu.VMEM),
        scratch_shapes=[
            pltpu.VMEM(maps.shape, jnp.float32),
            pltpu.VMEM(strip.shape, jnp.float32),
            pltpu.SMEM(weights.shape, jnp.float32),
            pltpu.SemaphoreType.DMA((2,)),
        ],
        compiler_params=pltpu.CompilerParams(vmem_limit_bytes=8 << 20),
    )(*[stay(x) for x in (weights, maps, *later)])
    for repeat in range(ITERS):
        tile = lax.all_to_all(mixes, "energy", split_axis=0, concat_axis=0, tiled=True)
        grads = patch_gradient(tile, probe, spots, counts, tables)
        grads = lax.all_to_all(grads, "energy", split_axis=0, concat_axis=0, tiled=True)
        current, to_far, to_near = on_chip(
            functools.partial(unmix_kernel, factor), (strip, part, part), (place, weights), (grads, current)
        )
        mine = with_edges(current, to_near, to_far, even)
        near, far = from_neighbours(mine)
        if repeat < ITERS - 1:
            current, mixes = on_chip(
                functools.partial(smooth_mix_kernel, last), (strip, spread), (place, weights), (mine, near, far), [field]
            )
    result = jax.ShapeDtypeStruct((planes, rows, columns), jnp.float32)
    out = on_chip(functools.partial(smooth_kernel, last), result, (place,), (mine, near, far), [field])
    return out.reshape(material_maps.shape)


def solution(mesh):
    in_specs = (
        P(None, None, "energy", "tile"),
        P(),
        P("energy", None, None),
        P("tile", None, None),
        P("energy", "tile", None, None, None),
    )
    out_specs = P(None, None, "energy", "tile")
    return jax.shard_map(shards, mesh=mesh, in_specs=in_specs, out_specs=out_specs, check_vma=False)
```

```python
import functools
import math

import jax
import jax.numpy as jnp
import numpy as np
from jax import lax
from jax.experimental import pallas as pl
from jax.experimental.pallas import tpu as pltpu
from jax.sharding import PartitionSpec as P

ITERS = 2
TV_STEPS = 3
DATA_STEP = 0.05
TV_STEP = 0.05
TV_EPS = 0.01

LEN = 128
GROUP = 16
LIMIT = 4096.0

def dft_tables(length):
    index = np.arange(length)
    angle = (index[:, None] * index[None, :] % length) * (-2.0 * math.pi / length)
    scale = 1.0 / math.sqrt(length)
    return tuple((wave(angle) * scale).astype(np.float32).astype(jnp.bfloat16) for wave in (np.cos, np.sin))


def dft_blocks(fr, fi):
    ahead = np.block([[fr, fi], [-fi, fr]])
    back = np.block([[fr, -fi], [fi, fr]])
    return jnp.asarray(ahead), jnp.asarray(back)


def dot(left, right):
    return jnp.dot(left, right, preferred_element_type=jnp.float32)

def pair_up(both):
    one, two = both
    return jnp.concatenate([
        jnp.concatenate([one[:, :LEN], two[:, :LEN]], 1),
        jnp.concatenate([one[:, LEN:], two[:, LEN:]], 1)], 0)

def sine_cosine(angle):
    turns = jnp.floor(angle * (2.0 / math.pi) + 0.5)
    rest = ((angle - turns * 1.5703125) - turns * 4.837512969970703125e-4) - turns * 7.54978995489188216e-8
    quadrant = turns.astype(jnp.int32)
    square = rest * rest
    sine = ((-1.9515295891e-4 * square + 8.3321608736e-3) * square - 1.6666654611e-1) * square * rest + rest
    cosine = ((2.443315711809948e-5 * square - 1.388731625493765e-3) * square + 4.166664568298827e-2) * square * square
    cosine = cosine - 0.5 * square + 1.0
    odd = (quadrant & 1) == 1
    first = jnp.where(odd, cosine, sine)
    second = jnp.where(odd, sine, cosine)
    return (
        jnp.where((quadrant & 2) == 2, -first, first),
        jnp.where(((quadrant + 1) & 2) == 2, -second, second),
    )


def patch_kernel(
    group, z_ref, spots_hbm, counts, probe_ref, ahead_ref, back_ref, out_ref, wave, total, spots, sem
):
    copy = pltpu.make_async_copy(spots_hbm, spots, sem)
    copy.start()
    patches = counts.shape[0]
    blocks = z_ref.shape[0]
    step = 4
    upper = lax.broadcasted_iota(jnp.int32, (step, 8, LEN), 1) < 4

    def parts(i, half):
        at = pl.multiple_of(i * step, step)
        rows = pl.ds(pl.multiple_of(i * step * 8, step * 8), step * 8)

        def part(c):
            low = z_ref[pl.ds(at, step), 8 * c + 4 * half : 8 * c + 4 * half + 8, :]
            high = z_ref[pl.ds(at, step), 8 * c + 4 * half + 12 : 8 * c + 4 * half + 20, :]
            return jnp.where(upper, low, high).reshape(step * 8, LEN)

        return rows, part(0), part(1)

    def expand(i, largest):
        for half in range(2):
            rows, size, angle = parts(i, half)
            growth = jnp.exp(size)
            sine, cosine = sine_cosine(angle)
            wave[half, rows, :] = growth * cosine
            wave[2 + half, rows, :] = growth * sine
            total[half, rows, :] = jnp.zeros((step * 8, LEN), jnp.float32)
            total[2 + half, rows, :] = jnp.zeros((step * 8, LEN), jnp.float32)
            largest = jnp.maximum(largest, jnp.abs(angle))
        return largest

    largest = lax.fori_loop(0, blocks // step, expand, jnp.zeros((step * 8, LEN), jnp.float32))

    @pl.when(jnp.max(largest) > LIMIT)
    def _():
        def again(i, carry):
            for half in range(2):
                rows, size, angle = parts(i, half)
                growth = jnp.exp(size)
                wave[half, rows, :] = growth * jnp.cos(angle)
                wave[2 + half, rows, :] = growth * jnp.sin(angle)
            return carry

        lax.fori_loop(0, blocks // step, again, 0)

    copy.wait()
    lane = lax.broadcasted_iota(jnp.int32, (LEN, LEN), 1)

    def one_group(g, carry):
        first = g * group
        exits = []
        for j in range(group):
            a = spots[0, first + j]
            b = spots[1, first + j]
            rows = pl.ds(a, LEN)
            keep = lane >= b
            shift = jnp.bitwise_and(LEN - b, LEN - 1)
            wr = pltpu.roll(jnp.where(keep, wave[0, rows, :], wave[1, rows, :]), shift, 1)
            wi = pltpu.roll(jnp.where(keep, wave[2, rows, :], wave[3, rows, :]), shift, 1)
            pr = probe_ref[:, :LEN]
            pi = probe_ref[:, LEN:]
            exits.append(jnp.concatenate([pr * wr - pi * wi, pr * wi + pi * wr], 1).astype(jnp.bfloat16))
        first_pass = dot(jnp.concatenate(exits, 0), ahead_ref[...]).astype(jnp.bfloat16)
        weighted = []
        for j in range(0, group, 2):
            far = dot(back_ref[...], pair_up([first_pass[k * LEN : (k + 1) * LEN] for k in (j, j + 1)]))
            for k in range(2):
                fr = far[:LEN, k * LEN : (k + 1) * LEN]
                fi = far[LEN:, k * LEN : (k + 1) * LEN]
                misfit = fr * fr + fi * fi - counts[first + j + k]
                weighted.append(jnp.concatenate([misfit * fr, misfit * fi], 1).astype(jnp.bfloat16))
        third_pass = dot(jnp.concatenate(weighted, 0), back_ref[...]).astype(jnp.bfloat16)
        for j in range(0, group, 2):
            grad = dot(ahead_ref[...], pair_up([third_pass[k * LEN : (k + 1) * LEN] for k in (j, j + 1)]))
            for k in range(2):
                a = spots[0, first + j + k]
                b = spots[1, first + j + k]
                rows = pl.ds(a, LEN)
                gr = grad[:LEN, k * LEN : (k + 1) * LEN]
                gi = grad[LEN:, k * LEN : (k + 1) * LEN]
                pr = probe_ref[:, :LEN]
                pi = probe_ref[:, LEN:]
                keep = lane >= b
                shift = jnp.bitwise_and(b, LEN - 1)
                ur = pltpu.roll(pr * gr + pi * gi, shift, 1)
                ui = pltpu.roll(pr * gi - pi * gr, shift, 1)
                total[0, rows, :] += jnp.where(keep, ur, 0.0)
                total[1, rows, :] += jnp.where(keep, 0.0, ur)
                total[2, rows, :] += jnp.where(keep, ui, 0.0)
                total[3, rows, :] += jnp.where(keep, 0.0, ui)
        return carry

    lax.fori_loop(0, patches // group, one_group, 0)

    def finish(i, carry):
        at = pl.multiple_of(i * step, step)
        rows = pl.ds(pl.multiple_of(i * step * 8, step * 8), step * 8)
        for half in range(2):
            orr = wave[half, rows, :]
            oi = wave[2 + half, rows, :]
            tr = total[half, rows, :]
            ti = total[2 + half, rows, :]
            for c, value in ((0, orr * tr + oi * ti), (1, orr * ti - oi * tr)):
                value = value.reshape(step, 8, LEN)
                lo = 8 * c + 4 * half
                out_ref[pl.ds(at, step), lo : lo + 4, :] = value[:, :4]
                out_ref[pl.ds(at, step), lo + 16 : lo + 20, :] = value[:, 4:]
        return carry

    lax.fori_loop(0, blocks // step, finish, 0)


def stay(array):
    return pltpu.with_memory_space_constraint(array, pltpu.HBM)


def patch_gradient(z, probe, spots, counts, tables, group=GROUP):
    strips = z.shape[0]
    vmem = pl.BlockSpec(memory_space=pltpu.VMEM)
    hbm = pl.BlockSpec(memory_space=pltpu.HBM)
    inputs = (counts, probe, *tables)
    out = pl.pallas_call(
        functools.partial(patch_kernel, group),
        out_shape=jax.ShapeDtypeStruct((strips // 2, 32, LEN), jnp.float32),
        in_specs=[vmem, hbm] + [vmem] * len(inputs),
        out_specs=vmem,
        scratch_shapes=[
            pltpu.VMEM((4, 4 * strips, LEN), jnp.float32),
            pltpu.VMEM((4, 4 * strips, LEN), jnp.float32),
            pltpu.SMEM(spots.shape, jnp.int32),
            pltpu.SemaphoreType.DMA,
        ],
        compiler_params=pltpu.CompilerParams(vmem_limit_bytes=16 << 20),
    )(z.reshape(strips // 2, 32, LEN), stay(spots), *inputs)
    return out.reshape(z.shape)


def mixed(planes, coefficient, out_ref):
    materials = len(planes) // 2

    def one(e, carry):
        re = jnp.zeros_like(planes[0])
        im = jnp.zeros_like(planes[0])
        for m in range(materials):
            cr = coefficient(2 * m, e)
            ci = coefficient(2 * m + 1, e)
            re = re + cr * planes[m] - ci * planes[materials + m]
            im = im + cr * planes[materials + m] + ci * planes[m]
        out_ref[e, 0:8, :] = re
        out_ref[e, 8:16, :] = im
        return carry

    lax.fori_loop(0, out_ref.shape[0], one, 0, unroll=8)


def mix_kernel(spectra_hbm, maps_hbm, *rest):
    out_ref, maps, rows_ref, spectra, sems = rest[-5:]
    copies = [
        pltpu.make_async_copy(spectra_hbm, spectra, sems.at[0]),
        pltpu.make_async_copy(maps_hbm, maps, sems.at[1]),
    ]
    for copy in copies:
        copy.start()
    for copy in copies:
        copy.wait()
    for half in range(2):
        rows_ref[:, 4 * half : 4 * half + 4, :] = maps[:, :, half * LEN : (half + 1) * LEN]
    mixed([rows_ref[p] for p in range(rows_ref.shape[0])], lambda k, e: spectra[k, e], out_ref)


def unmix_kernel(factor, grads_ref, rows_ref, spectra, out_ref, far_ref, near_ref):
    materials = rows_ref.shape[0] // 2

    def one(e, sums):
        gr = grads_ref[e, 0:8, :]
        gi = grads_ref[e, 8:16, :]
        reals, imags = [], []
        for m in range(materials):
            cr = spectra[2 * m, pl.ds(e, 1), :]
            ci = spectra[2 * m + 1, pl.ds(e, 1), :]
            reals.append(sums[m] + cr * gr + ci * gi)
            imags.append(sums[materials + m] + cr * gi - ci * gr)
        return tuple(reals + imags)

    even = lax.axis_index("tile") % 2 == 0
    zero = jnp.zeros(rows_ref.shape[1:], jnp.float32)
    sums = lax.fori_loop(0, grads_ref.shape[0], one, (zero,) * (2 * materials), unroll=8)
    for p in range(2 * materials):
        value = rows_ref[p] - factor * sums[p]
        out_ref[p] = value
        near_ref[p] = jnp.where(even, value[4:], value[:4])
        far_ref[p] = jnp.where(even, value[:4], value[4:])


def smooth(last, mine_ref, near_ref, far_ref, field):
    planes = field.shape[0]
    place = (lax.axis_index("energy"), lax.axis_index("tile"))
    even = place[0] % 2 == 0
    for p in range(planes):
        for j in range(3):
            rows = slice(8 * p + 4 * j, 8 * p + 4 * j + 4) if j < 2 else slice(8 * planes + 4 * p, 8 * planes + 4 * p + 4)
            lanes = slice(j * LEN, (j + 1) * LEN)
            near = near_ref[rows, :]
            far = far_ref[rows, :]
            field[p, 0:4, lanes] = jnp.where(even, far, near)
            field[p, 4:8, lanes] = mine_ref[rows, :]
            field[p, 8:12, lanes] = jnp.where(even, near, far)
            field[p, 12:16, lanes] = jnp.zeros((4, LEN), jnp.float32)
    shape = (16, 3 * LEN)
    row = lax.broadcasted_iota(jnp.int32, shape, 0)
    lane = lax.broadcasted_iota(jnp.int32, shape, 1)
    low_row = jnp.where(place[0] == 0, 4, 0)
    high_row = jnp.where(place[0] == last[0], 8, 16)
    low_edge = jnp.where(place[1] == last[1], 2 * LEN + LEN // 2, 0)
    high_edge = jnp.where(place[1] == 0, 2 * LEN + LEN // 2, 3 * LEN)
    inside = (row >= low_row) & (row < high_row)
    inside = inside & ((lane < 2 * LEN) | ((lane >= low_edge) & (lane < high_edge)))
    results = [None] * planes
    for m in range(planes // 2):
        pair = [jnp.where(inside, field[p], 0.0) for p in (m, planes // 2 + m)]
        for _ in range(TV_STEPS):
            down = [pltpu.roll(x, 15, 0) - x for x in pair]
            across = [pltpu.roll(x, 3 * LEN - 1, 1) - x for x in pair]
            square = down[0] * down[0] + across[0] * across[0] + down[1] * down[1] + across[1] * across[1]
            scale = lax.rsqrt(square + TV_EPS)
            fresh = []
            for x, d, c in zip(pair, down, across):
                d = d * scale
                c = c * scale
                moved = x + TV_STEP * (d - pltpu.roll(d, 1, 0) + c - pltpu.roll(c, 1, 1))
                fresh.append(jnp.where(inside, moved, 0.0))
            pair = fresh
        results[m], results[planes // 2 + m] = pair
    return results


def smooth_mix_kernel(last, mine_ref, near_ref, far_ref, spectra, rows_ref, out_ref, field):
    results = smooth(last, mine_ref, near_ref, far_ref, field)
    for p, value in enumerate(results):
        rows_ref[p, 0:4, :] = value[4:8, :LEN]
        rows_ref[p, 4:8, :] = value[4:8, LEN : 2 * LEN]
    mixed([rows_ref[p] for p in range(rows_ref.shape[0])], lambda k, e: spectra[k, pl.ds(e, 1), :], out_ref)


def smooth_kernel(last, mine_ref, near_ref, far_ref, out_ref, field):
    results = smooth(last, mine_ref, near_ref, far_ref, field)
    for p, value in enumerate(results):
        out_ref[p] = value[4:8, : 2 * LEN]


def on_chip(kernel, out_shape, arrays, scratch=()):
    vmem = pl.BlockSpec(memory_space=pltpu.VMEM)
    return pl.pallas_call(
        kernel,
        out_shape=out_shape,
        in_specs=[vmem] * len(arrays),
        out_specs=jax.tree.map(lambda _: vmem, out_shape),
        scratch_shapes=list(scratch),
        compiler_params=pltpu.CompilerParams(vmem_limit_bytes=8 << 20),
    )(*arrays)


def swaps(axis):
    count = lax.axis_size(axis)
    near = [(i, i ^ 1) for i in range(count)]
    return near, [((i + 1) % count, (k + 1) % count) for i, k in near]


def with_edges(rows, to_near, to_far, even):
    near, far = swaps("tile")
    from_far = lax.ppermute(to_far, "tile", far)
    from_near = lax.ppermute(to_near, "tile", near)
    lane = lax.broadcasted_iota(jnp.int32, from_near.shape, 2)
    edges = jnp.where((lane < LEN // 2) != even, from_far, from_near)
    return jnp.concatenate([rows.reshape(-1, LEN), edges.reshape(-1, LEN)], 0)


def from_neighbours(strip):
    near, far = swaps("energy")
    return lax.ppermute(strip, "energy", near), lax.ppermute(strip, "energy", far)


def shards(material_maps, spectra, probes, offsets, measured):
    energies, materials, _ = spectra.shape
    planes = 2 * materials
    rows, columns = material_maps.shape[2:]
    assert rows == 4 and columns == 2 * LEN
    probe = probes[0]
    spots = offsets[0].T
    counts = measured[0, 0]
    tables = dft_blocks(*dft_tables(LEN))
    weights = spectra.transpose(1, 2, 0).reshape(2 * materials, energies)
    factor = DATA_STEP / math.sqrt(energies)
    spread_weights = jnp.broadcast_to(weights[:, :, None], (*weights.shape, LEN))
    last = (lax.axis_size("energy") - 1, lax.axis_size("tile") - 1)
    strip = jax.ShapeDtypeStruct((planes, 2 * rows, LEN), jnp.float32)
    part = jax.ShapeDtypeStruct((planes, rows, LEN), jnp.float32)
    spread = jax.ShapeDtypeStruct((energies, 4 * rows, LEN), jnp.float32)
    field = pltpu.VMEM((planes, 16, 3 * LEN), jnp.float32)
    even = lax.axis_index("tile") % 2 == 0
    maps, even, spread_weights = lax.optimization_barrier(
        (material_maps.reshape(planes, rows, columns), even, spread_weights)
    )
    current = maps.reshape(planes, rows, 2, LEN).transpose(0, 2, 1, 3).reshape(planes, 2 * rows, LEN)
    hbm = pl.BlockSpec(memory_space=pltpu.HBM)
    later = (counts, probe, *tables)
    mixes = pl.pallas_call(
        mix_kernel,
        out_shape=spread,
        in_specs=[hbm] * (2 + len(later)),
        out_specs=pl.BlockSpec(memory_space=pltpu.VMEM),
        scratch_shapes=[
            pltpu.VMEM(maps.shape, jnp.float32),
            pltpu.VMEM(strip.shape, jnp.float32),
            pltpu.SMEM(weights.shape, jnp.float32),
            pltpu.SemaphoreType.DMA((2,)),
        ],
        compiler_params=pltpu.CompilerParams(vmem_limit_bytes=8 << 20),
    )(*[stay(x) for x in (weights, maps, *later)])
    for repeat in range(ITERS):
        tile = lax.all_to_all(mixes, "energy", split_axis=0, concat_axis=0, tiled=True)
        grads = patch_gradient(tile, probe, spots, counts, tables)
        grads = lax.all_to_all(grads, "energy", split_axis=0, concat_axis=0, tiled=True)
        current, to_far, to_near = on_chip(
            functools.partial(unmix_kernel, factor), (strip, part, part), (grads, current, spread_weights)
        )
        mine = with_edges(current, to_near, to_far, even)
        near, far = from_neighbours(mine)
        if repeat < ITERS - 1:
            current, mixes = on_chip(
                functools.partial(smooth_mix_kernel, last), (strip, spread), (mine, near, far, spread_weights), [field]
            )
    result = jax.ShapeDtypeStruct((planes, rows, columns), jnp.float32)
    out = on_chip(functools.partial(smooth_kernel, last), result, (mine, near, far), [field])
    return out.reshape(material_maps.shape)


def solution(mesh):
    in_specs = (
        P(None, None, "energy", "tile"),
        P(),
        P("energy", None, None),
        P("tile", None, None),
        P("energy", "tile", None, None, None),
    )
    out_specs = P(None, None, "energy", "tile")
    return jax.shard_map(shards, mesh=mesh, in_specs=in_specs, out_specs=out_specs, check_vma=False)
```

```python
import functools
import math

import jax
import jax.numpy as jnp
import numpy as np
from jax import lax
from jax.experimental import pallas as pl
from jax.experimental.pallas import tpu as pltpu
from jax.sharding import PartitionSpec as P

ITERS = 2
TV_STEPS = 3
DATA_STEP = 0.05
TV_STEP = 0.05
TV_EPS = 0.01

LEN = 128
GROUP = 16
LIMIT = 4096.0

def dft_tables(length):
    index = np.arange(length)
    angle = (index[:, None] * index[None, :] % length) * (-2.0 * math.pi / length)
    scale = 1.0 / math.sqrt(length)
    return tuple((wave(angle) * scale).astype(np.float32).astype(jnp.bfloat16) for wave in (np.cos, np.sin))


def dft_blocks(fr, fi):
    ahead = np.block([[fr, fi], [-fi, fr]])
    back = np.block([[fr, -fi], [fi, fr]])
    return jnp.asarray(ahead), jnp.asarray(back)


def dot(left, right):
    return jnp.dot(left, right, preferred_element_type=jnp.float32)

def pair_up(both):
    one, two = both
    return jnp.concatenate([
        jnp.concatenate([one[:, :LEN], two[:, :LEN]], 1),
        jnp.concatenate([one[:, LEN:], two[:, LEN:]], 1)], 0)

def sine_cosine(angle):
    turns = jnp.floor(angle * (2.0 / math.pi) + 0.5)
    rest = ((angle - turns * 1.5703125) - turns * 4.837512969970703125e-4) - turns * 7.54978995489188216e-8
    quadrant = turns.astype(jnp.int32)
    square = rest * rest
    sine = ((-1.9515295891e-4 * square + 8.3321608736e-3) * square - 1.6666654611e-1) * square * rest + rest
    cosine = ((2.443315711809948e-5 * square - 1.388731625493765e-3) * square + 4.166664568298827e-2) * square * square
    cosine = cosine - 0.5 * square + 1.0
    odd = (quadrant & 1) == 1
    first = jnp.where(odd, cosine, sine)
    second = jnp.where(odd, sine, cosine)
    return (
        jnp.where((quadrant & 2) == 2, -first, first),
        jnp.where(((quadrant + 1) & 2) == 2, -second, second),
    )


def patch_kernel(
    group, z_ref, spots_hbm, counts, probe_ref, ahead_ref, back_ref, out_ref, wave, total, spots, sem
):
    copy = pltpu.make_async_copy(spots_hbm, spots, sem)
    copy.start()
    patches = counts.shape[0]
    blocks = z_ref.shape[0]
    step = 4
    upper = lax.broadcasted_iota(jnp.int32, (step, 8, LEN), 1) < 4

    def parts(i, half):
        at = pl.multiple_of(i * step, step)
        rows = pl.ds(pl.multiple_of(i * step * 8, step * 8), step * 8)

        def part(c):
            low = z_ref[pl.ds(at, step), 8 * c + 4 * half : 8 * c + 4 * half + 8, :]
            high = z_ref[pl.ds(at, step), 8 * c + 4 * half + 12 : 8 * c + 4 * half + 20, :]
            return jnp.where(upper, low, high).reshape(step * 8, LEN)

        return rows, part(0), part(1)

    def expand(i, largest):
        for half in range(2):
            rows, size, angle = parts(i, half)
            growth = jnp.exp(size)
            sine, cosine = sine_cosine(angle)
            wave[half, rows, :] = growth * cosine
            wave[2 + half, rows, :] = growth * sine
            total[half, rows, :] = jnp.zeros((step * 8, LEN), jnp.float32)
            total[2 + half, rows, :] = jnp.zeros((step * 8, LEN), jnp.float32)
            largest = jnp.maximum(largest, jnp.abs(angle))
        return largest

    largest = lax.fori_loop(0, blocks // step, expand, jnp.zeros((step * 8, LEN), jnp.float32))

    @pl.when(jnp.max(largest) > LIMIT)
    def _():
        def again(i, carry):
            for half in range(2):
                rows, size, angle = parts(i, half)
                growth = jnp.exp(size)
                wave[half, rows, :] = growth * jnp.cos(angle)
                wave[2 + half, rows, :] = growth * jnp.sin(angle)
            return carry

        lax.fori_loop(0, blocks // step, again, 0)

    copy.wait()
    lane = lax.broadcasted_iota(jnp.int32, (LEN, LEN), 1)

    def one_group(g, carry):
        first = g * group
        exits = []
        for j in range(group):
            a = spots[0, first + j]
            b = spots[1, first + j]
            rows = pl.ds(a, LEN)
            keep = lane >= b
            shift = jnp.bitwise_and(LEN - b, LEN - 1)
            wr = pltpu.roll(jnp.where(keep, wave[0, rows, :], wave[1, rows, :]), shift, 1)
            wi = pltpu.roll(jnp.where(keep, wave[2, rows, :], wave[3, rows, :]), shift, 1)
            pr = probe_ref[:, :LEN]
            pi = probe_ref[:, LEN:]
            exits.append(jnp.concatenate([pr * wr - pi * wi, pr * wi + pi * wr], 1).astype(jnp.bfloat16))
        first_pass = dot(jnp.concatenate(exits, 0), ahead_ref[...]).astype(jnp.bfloat16)
        weighted = []
        for j in range(0, group, 2):
            far = dot(back_ref[...], pair_up([first_pass[k * LEN : (k + 1) * LEN] for k in (j, j + 1)]))
            for k in range(2):
                fr = far[:LEN, k * LEN : (k + 1) * LEN]
                fi = far[LEN:, k * LEN : (k + 1) * LEN]
                misfit = fr * fr + fi * fi - counts[first + j + k]
                weighted.append(jnp.concatenate([misfit * fr, misfit * fi], 1).astype(jnp.bfloat16))
        third_pass = dot(jnp.concatenate(weighted, 0), back_ref[...]).astype(jnp.bfloat16)
        for j in range(0, group, 2):
            grad = dot(ahead_ref[...], pair_up([third_pass[k * LEN : (k + 1) * LEN] for k in (j, j + 1)]))
            for k in range(2):
                a = spots[0, first + j + k]
                b = spots[1, first + j + k]
                rows = pl.ds(a, LEN)
                gr = grad[:LEN, k * LEN : (k + 1) * LEN]
                gi = grad[LEN:, k * LEN : (k + 1) * LEN]
                pr = probe_ref[:, :LEN]
                pi = probe_ref[:, LEN:]
                keep = lane >= b
                shift = jnp.bitwise_and(b, LEN - 1)
                ur = pltpu.roll(pr * gr + pi * gi, shift, 1)
                ui = pltpu.roll(pr * gi - pi * gr, shift, 1)
                total[0, rows, :] += jnp.where(keep, ur, 0.0)
                total[1, rows, :] += jnp.where(keep, 0.0, ur)
                total[2, rows, :] += jnp.where(keep, ui, 0.0)
                total[3, rows, :] += jnp.where(keep, 0.0, ui)
        return carry

    lax.fori_loop(0, patches // group, one_group, 0)

    def finish(i, carry):
        at = pl.multiple_of(i * step, step)
        rows = pl.ds(pl.multiple_of(i * step * 8, step * 8), step * 8)
        for half in range(2):
            orr = wave[half, rows, :]
            oi = wave[2 + half, rows, :]
            tr = total[half, rows, :]
            ti = total[2 + half, rows, :]
            for c, value in ((0, orr * tr + oi * ti), (1, orr * ti - oi * tr)):
                value = value.reshape(step, 8, LEN)
                lo = 8 * c + 4 * half
                out_ref[pl.ds(at, step), lo : lo + 4, :] = value[:, :4]
                out_ref[pl.ds(at, step), lo + 16 : lo + 20, :] = value[:, 4:]
        return carry

    lax.fori_loop(0, blocks // step, finish, 0)


def stay(array):
    return pltpu.with_memory_space_constraint(array, pltpu.HBM)


def patch_gradient(z, probe, spots, counts, tables, group=GROUP):
    strips = z.shape[0]
    vmem = pl.BlockSpec(memory_space=pltpu.VMEM)
    hbm = pl.BlockSpec(memory_space=pltpu.HBM)
    inputs = (counts, probe, *tables)
    out = pl.pallas_call(
        functools.partial(patch_kernel, group),
        out_shape=jax.ShapeDtypeStruct((strips // 2, 32, LEN), jnp.float32),
        in_specs=[vmem, hbm] + [vmem] * len(inputs),
        out_specs=vmem,
        scratch_shapes=[
            pltpu.VMEM((4, 4 * strips, LEN), jnp.float32),
            pltpu.VMEM((4, 4 * strips, LEN), jnp.float32),
            pltpu.SMEM(spots.shape, jnp.int32),
            pltpu.SemaphoreType.DMA,
        ],
        compiler_params=pltpu.CompilerParams(vmem_limit_bytes=16 << 20),
    )(z.reshape(strips // 2, 32, LEN), stay(spots), *inputs)
    return out.reshape(z.shape)


def mixed(planes, coefficient, out_ref):
    materials = len(planes) // 2

    def one(e, carry):
        re = jnp.zeros_like(planes[0])
        im = jnp.zeros_like(planes[0])
        for m in range(materials):
            cr = coefficient(2 * m, e)
            ci = coefficient(2 * m + 1, e)
            re = re + cr * planes[m] - ci * planes[materials + m]
            im = im + cr * planes[materials + m] + ci * planes[m]
        out_ref[e, 0:8, :] = re
        out_ref[e, 8:16, :] = im
        return carry

    lax.fori_loop(0, out_ref.shape[0], one, 0, unroll=8)


def mix_kernel(spectra_hbm, maps_hbm, *rest):
    out_ref, rows_of, maps, rows_ref, spectra, sems = rest[-6:]
    copies = [
        pltpu.make_async_copy(spectra_hbm, spectra, sems.at[0]),
        pltpu.make_async_copy(maps_hbm, maps, sems.at[1]),
    ]
    for copy in copies:
        copy.start()
    for copy in copies:
        copy.wait()
    for half in range(2):
        rows_ref[:, 4 * half : 4 * half + 4, :] = maps[:, :, half * LEN : (half + 1) * LEN]

    def spread(e, carry):
        for k in range(spectra.shape[0]):
            rows_of[k, pl.ds(e, 1), :] = jnp.full((1, LEN), spectra[k, e])
        return carry

    lax.fori_loop(0, out_ref.shape[0], spread, 0, unroll=8)
    mixed([rows_ref[p] for p in range(rows_ref.shape[0])], lambda k, e: spectra[k, e], out_ref)


def unmix_kernel(factor, grads_ref, rows_ref, spectra, out_ref, far_ref, near_ref):
    materials = rows_ref.shape[0] // 2

    def one(e, sums):
        gr = grads_ref[e, 0:8, :]
        gi = grads_ref[e, 8:16, :]
        reals, imags = [], []
        for m in range(materials):
            cr = spectra[2 * m, pl.ds(e, 1), :]
            ci = spectra[2 * m + 1, pl.ds(e, 1), :]
            reals.append(sums[m] + cr * gr + ci * gi)
            imags.append(sums[materials + m] + cr * gi - ci * gr)
        return tuple(reals + imags)

    even = lax.axis_index("tile") % 2 == 0
    zero = jnp.zeros(rows_ref.shape[1:], jnp.float32)
    sums = lax.fori_loop(0, grads_ref.shape[0], one, (zero,) * (2 * materials), unroll=8)
    for p in range(2 * materials):
        value = rows_ref[p] - factor * sums[p]
        out_ref[p] = value
        near_ref[p] = jnp.where(even, value[4:], value[:4])
        far_ref[p] = jnp.where(even, value[:4], value[4:])


def smooth(last, mine_ref, near_ref, far_ref, field):
    planes = field.shape[0]
    place = (lax.axis_index("energy"), lax.axis_index("tile"))
    even = place[0] % 2 == 0
    for p in range(planes):
        for j in range(3):
            rows = slice(8 * p + 4 * j, 8 * p + 4 * j + 4) if j < 2 else slice(8 * planes + 4 * p, 8 * planes + 4 * p + 4)
            lanes = slice(j * LEN, (j + 1) * LEN)
            near = near_ref[rows, :]
            far = far_ref[rows, :]
            field[p, 0:4, lanes] = jnp.where(even, far, near)
            field[p, 4:8, lanes] = mine_ref[rows, :]
            field[p, 8:12, lanes] = jnp.where(even, near, far)
            field[p, 12:16, lanes] = jnp.zeros((4, LEN), jnp.float32)
    shape = (16, 3 * LEN)
    row = lax.broadcasted_iota(jnp.int32, shape, 0)
    lane = lax.broadcasted_iota(jnp.int32, shape, 1)
    low_row = jnp.where(place[0] == 0, 4, 0)
    high_row = jnp.where(place[0] == last[0], 8, 16)
    low_edge = jnp.where(place[1] == last[1], 2 * LEN + LEN // 2, 0)
    high_edge = jnp.where(place[1] == 0, 2 * LEN + LEN // 2, 3 * LEN)
    inside = (row >= low_row) & (row < high_row)
    inside = inside & ((lane < 2 * LEN) | ((lane >= low_edge) & (lane < high_edge)))
    results = [None] * planes
    for m in range(planes // 2):
        pair = [jnp.where(inside, field[p], 0.0) for p in (m, planes // 2 + m)]
        for _ in range(TV_STEPS):
            down = [pltpu.roll(x, 15, 0) - x for x in pair]
            across = [pltpu.roll(x, 3 * LEN - 1, 1) - x for x in pair]
            square = down[0] * down[0] + across[0] * across[0] + down[1] * down[1] + across[1] * across[1]
            scale = lax.rsqrt(square + TV_EPS)
            fresh = []
            for x, d, c in zip(pair, down, across):
                d = d * scale
                c = c * scale
                moved = x + TV_STEP * (d - pltpu.roll(d, 1, 0) + c - pltpu.roll(c, 1, 1))
                fresh.append(jnp.where(inside, moved, 0.0))
            pair = fresh
        results[m], results[planes // 2 + m] = pair
    return results


def smooth_mix_kernel(last, mine_ref, near_ref, far_ref, spectra, rows_ref, out_ref, field):
    results = smooth(last, mine_ref, near_ref, far_ref, field)
    for p, value in enumerate(results):
        rows_ref[p, 0:4, :] = value[4:8, :LEN]
        rows_ref[p, 4:8, :] = value[4:8, LEN : 2 * LEN]
    mixed([rows_ref[p] for p in range(rows_ref.shape[0])], lambda k, e: spectra[k, pl.ds(e, 1), :], out_ref)


def smooth_kernel(last, mine_ref, near_ref, far_ref, out_ref, field):
    results = smooth(last, mine_ref, near_ref, far_ref, field)
    for p, value in enumerate(results):
        out_ref[p] = value[4:8, : 2 * LEN]


def on_chip(kernel, out_shape, arrays, scratch=()):
    vmem = pl.BlockSpec(memory_space=pltpu.VMEM)
    return pl.pallas_call(
        kernel,
        out_shape=out_shape,
        in_specs=[vmem] * len(arrays),
        out_specs=jax.tree.map(lambda _: vmem, out_shape),
        scratch_shapes=list(scratch),
        compiler_params=pltpu.CompilerParams(vmem_limit_bytes=8 << 20),
    )(*arrays)


def swaps(axis):
    count = lax.axis_size(axis)
    near = [(i, i ^ 1) for i in range(count)]
    return near, [((i + 1) % count, (k + 1) % count) for i, k in near]


def with_edges(rows, to_near, to_far, even):
    near, far = swaps("tile")
    from_far = lax.ppermute(to_far, "tile", far)
    from_near = lax.ppermute(to_near, "tile", near)
    lane = lax.broadcasted_iota(jnp.int32, from_near.shape, 2)
    edges = jnp.where((lane < LEN // 2) != even, from_far, from_near)
    return jnp.concatenate([rows.reshape(-1, LEN), edges.reshape(-1, LEN)], 0)


def from_neighbours(strip):
    near, far = swaps("energy")
    return lax.ppermute(strip, "energy", near), lax.ppermute(strip, "energy", far)


def shards(material_maps, spectra, probes, offsets, measured):
    energies, materials, _ = spectra.shape
    planes = 2 * materials
    rows, columns = material_maps.shape[2:]
    assert rows == 4 and columns == 2 * LEN
    probe = probes[0]
    spots = offsets[0].T
    counts = measured[0, 0]
    tables = dft_blocks(*dft_tables(LEN))
    weights = spectra.transpose(1, 2, 0).reshape(2 * materials, energies)
    factor = DATA_STEP / math.sqrt(energies)
    last = (lax.axis_size("energy") - 1, lax.axis_size("tile") - 1)
    strip = jax.ShapeDtypeStruct((planes, 2 * rows, LEN), jnp.float32)
    part = jax.ShapeDtypeStruct((planes, rows, LEN), jnp.float32)
    spread = jax.ShapeDtypeStruct((energies, 4 * rows, LEN), jnp.float32)
    field = pltpu.VMEM((planes, 16, 3 * LEN), jnp.float32)
    even = lax.axis_index("tile") % 2 == 0
    maps, even = lax.optimization_barrier((material_maps.reshape(planes, rows, columns), even))
    current = maps.reshape(planes, rows, 2, LEN).transpose(0, 2, 1, 3).reshape(planes, 2 * rows, LEN)
    hbm = pl.BlockSpec(memory_space=pltpu.HBM)
    later = (counts, probe, *tables)
    mixes, spread_weights = pl.pallas_call(
        mix_kernel,
        out_shape=(spread, jax.ShapeDtypeStruct((*weights.shape, LEN), jnp.float32)),
        in_specs=[hbm] * (2 + len(later)),
        out_specs=(pl.BlockSpec(memory_space=pltpu.VMEM),) * 2,
        scratch_shapes=[
            pltpu.VMEM(maps.shape, jnp.float32),
            pltpu.VMEM(strip.shape, jnp.float32),
            pltpu.SMEM(weights.shape, jnp.float32),
            pltpu.SemaphoreType.DMA((2,)),
        ],
        compiler_params=pltpu.CompilerParams(vmem_limit_bytes=8 << 20),
    )(*[stay(x) for x in (weights, maps, *later)])
    for repeat in range(ITERS):
        tile = lax.all_to_all(mixes, "energy", split_axis=0, concat_axis=0, tiled=True)
        grads = patch_gradient(tile, probe, spots, counts, tables)
        grads = lax.all_to_all(grads, "energy", split_axis=0, concat_axis=0, tiled=True)
        current, to_far, to_near = on_chip(
            functools.partial(unmix_kernel, factor), (strip, part, part), (grads, current, spread_weights)
        )
        mine = with_edges(current, to_near, to_far, even)
        near, far = from_neighbours(mine)
        if repeat < ITERS - 1:
            current, mixes = on_chip(
                functools.partial(smooth_mix_kernel, last), (strip, spread), (mine, near, far, spread_weights), [field]
            )
    result = jax.ShapeDtypeStruct((planes, rows, columns), jnp.float32)
    out = on_chip(functools.partial(smooth_kernel, last), result, (mine, near, far), [field])
    return out.reshape(material_maps.shape)


def solution(mesh):
    in_specs = (
        P(None, None, "energy", "tile"),
        P(),
        P("energy", None, None),
        P("tile", None, None),
        P("energy", "tile", None, None, None),
    )
    out_specs = P(None, None, "energy", "tile")
    return jax.shard_map(shards, mesh=mesh, in_specs=in_specs, out_specs=out_specs, check_vma=False)
```

```python
import functools
import math

import jax
import jax.numpy as jnp
import numpy as np
from jax import lax
from jax.experimental import pallas as pl
from jax.experimental.pallas import tpu as pltpu
from jax.sharding import PartitionSpec as P

ITERS = 2
TV_STEPS = 3
DATA_STEP = 0.05
TV_STEP = 0.05
TV_EPS = 0.01

LEN = 128
GROUP = 16
LIMIT = 4096.0

def dft_tables(length):
    index = np.arange(length)
    angle = (index[:, None] * index[None, :] % length) * (-2.0 * math.pi / length)
    scale = 1.0 / math.sqrt(length)
    return tuple((wave(angle) * scale).astype(np.float32).astype(jnp.bfloat16) for wave in (np.cos, np.sin))


def dft_blocks(fr, fi):
    ahead = np.block([[fr, fi], [-fi, fr]])
    back = np.block([[fr, -fi], [fi, fr]])
    return jnp.asarray(ahead), jnp.asarray(back)


def dot(left, right):
    return jnp.dot(left, right, preferred_element_type=jnp.float32)

def pair_up(both):
    one, two = both
    return jnp.concatenate([
        jnp.concatenate([one[:, :LEN], two[:, :LEN]], 1),
        jnp.concatenate([one[:, LEN:], two[:, LEN:]], 1)], 0)

def sine_cosine(angle):
    turns = jnp.floor(angle * (2.0 / math.pi) + 0.5)
    rest = ((angle - turns * 1.5703125) - turns * 4.837512969970703125e-4) - turns * 7.54978995489188216e-8
    quadrant = turns.astype(jnp.int32)
    square = rest * rest
    sine = ((-1.9515295891e-4 * square + 8.3321608736e-3) * square - 1.6666654611e-1) * square * rest + rest
    cosine = ((2.443315711809948e-5 * square - 1.388731625493765e-3) * square + 4.166664568298827e-2) * square * square
    cosine = cosine - 0.5 * square + 1.0
    odd = (quadrant & 1) == 1
    first = jnp.where(odd, cosine, sine)
    second = jnp.where(odd, sine, cosine)
    return (
        jnp.where((quadrant & 2) == 2, -first, first),
        jnp.where(((quadrant + 1) & 2) == 2, -second, second),
    )


def patch_kernel(
    group, z_ref, spots_hbm, counts, probe_ref, ahead_ref, back_ref, out_ref, wave, total, spots, sem
):
    copy = pltpu.make_async_copy(spots_hbm, spots, sem)
    copy.start()
    patches = counts.shape[0]
    blocks = z_ref.shape[0]
    step = 4
    upper = lax.broadcasted_iota(jnp.int32, (step, 8, LEN), 1) < 4

    def parts(i, half):
        at = pl.multiple_of(i * step, step)
        rows = pl.ds(pl.multiple_of(i * step * 8, step * 8), step * 8)

        def part(c):
            low = z_ref[pl.ds(at, step), 8 * c + 4 * half : 8 * c + 4 * half + 8, :]
            high = z_ref[pl.ds(at, step), 8 * c + 4 * half + 12 : 8 * c + 4 * half + 20, :]
            return jnp.where(upper, low, high).reshape(step * 8, LEN)

        return rows, part(0), part(1)

    def expand(i, largest):
        for half in range(2):
            rows, size, angle = parts(i, half)
            growth = jnp.exp(size)
            sine, cosine = sine_cosine(angle)
            wave[half, rows, :] = growth * cosine
            wave[2 + half, rows, :] = growth * sine
            total[half, rows, :] = jnp.zeros((step * 8, LEN), jnp.float32)
            total[2 + half, rows, :] = jnp.zeros((step * 8, LEN), jnp.float32)
            largest = jnp.maximum(largest, jnp.abs(angle))
        return largest

    largest = lax.fori_loop(0, blocks // step, expand, jnp.zeros((step * 8, LEN), jnp.float32))

    @pl.when(jnp.max(largest) > LIMIT)
    def _():
        def again(i, carry):
            for half in range(2):
                rows, size, angle = parts(i, half)
                growth = jnp.exp(size)
                wave[half, rows, :] = growth * jnp.cos(angle)
                wave[2 + half, rows, :] = growth * jnp.sin(angle)
            return carry

        lax.fori_loop(0, blocks // step, again, 0)

    copy.wait()
    lane = lax.broadcasted_iota(jnp.int32, (LEN, LEN), 1)

    def one_group(g, carry):
        first = g * group
        exits = []
        for j in range(group):
            a = spots[0, first + j]
            b = spots[1, first + j]
            rows = pl.ds(a, LEN)
            keep = lane >= b
            shift = jnp.bitwise_and(LEN - b, LEN - 1)
            wr = pltpu.roll(jnp.where(keep, wave[0, rows, :], wave[1, rows, :]), shift, 1)
            wi = pltpu.roll(jnp.where(keep, wave[2, rows, :], wave[3, rows, :]), shift, 1)
            pr = probe_ref[:, :LEN]
            pi = probe_ref[:, LEN:]
            exits.append(jnp.concatenate([pr * wr - pi * wi, pr * wi + pi * wr], 1).astype(jnp.bfloat16))
        first_pass = dot(jnp.concatenate(exits, 0), ahead_ref[...]).astype(jnp.bfloat16)
        weighted = []
        for j in range(0, group, 2):
            far = dot(back_ref[...], pair_up([first_pass[k * LEN : (k + 1) * LEN] for k in (j, j + 1)]))
            for k in range(2):
                fr = far[:LEN, k * LEN : (k + 1) * LEN]
                fi = far[LEN:, k * LEN : (k + 1) * LEN]
                misfit = fr * fr + fi * fi - counts[first + j + k]
                weighted.append(jnp.concatenate([misfit * fr, misfit * fi], 1).astype(jnp.bfloat16))
        third_pass = dot(jnp.concatenate(weighted, 0), back_ref[...]).astype(jnp.bfloat16)
        for j in range(0, group, 2):
            grad = dot(ahead_ref[...], pair_up([third_pass[k * LEN : (k + 1) * LEN] for k in (j, j + 1)]))
            for k in range(2):
                a = spots[0, first + j + k]
                b = spots[1, first + j + k]
                rows = pl.ds(a, LEN)
                gr = grad[:LEN, k * LEN : (k + 1) * LEN]
                gi = grad[LEN:, k * LEN : (k + 1) * LEN]
                pr = probe_ref[:, :LEN]
                pi = probe_ref[:, LEN:]
                keep = lane >= b
                shift = jnp.bitwise_and(b, LEN - 1)
                ur = pltpu.roll(pr * gr + pi * gi, shift, 1)
                ui = pltpu.roll(pr * gi - pi * gr, shift, 1)
                total[0, rows, :] += jnp.where(keep, ur, 0.0)
                total[1, rows, :] += jnp.where(keep, 0.0, ur)
                total[2, rows, :] += jnp.where(keep, ui, 0.0)
                total[3, rows, :] += jnp.where(keep, 0.0, ui)
        return carry

    lax.fori_loop(0, patches // group, one_group, 0)

    def finish(i, carry):
        at = pl.multiple_of(i * step, step)
        rows = pl.ds(pl.multiple_of(i * step * 8, step * 8), step * 8)
        for half in range(2):
            orr = wave[half, rows, :]
            oi = wave[2 + half, rows, :]
            tr = total[half, rows, :]
            ti = total[2 + half, rows, :]
            for c, value in ((0, orr * tr + oi * ti), (1, orr * ti - oi * tr)):
                value = value.reshape(step, 8, LEN)
                lo = 8 * c + 4 * half
                out_ref[pl.ds(at, step), lo : lo + 4, :] = value[:, :4]
                out_ref[pl.ds(at, step), lo + 16 : lo + 20, :] = value[:, 4:]
        return carry

    lax.fori_loop(0, blocks // step, finish, 0)


def stay(array):
    return pltpu.with_memory_space_constraint(array, pltpu.HBM)


def patch_gradient(z, probe, spots, counts, tables, group=GROUP):
    strips = z.shape[0]
    vmem = pl.BlockSpec(memory_space=pltpu.VMEM)
    hbm = pl.BlockSpec(memory_space=pltpu.HBM)
    inputs = (counts, probe, *tables)
    out = pl.pallas_call(
        functools.partial(patch_kernel, group),
        out_shape=jax.ShapeDtypeStruct((strips // 2, 32, LEN), jnp.float32),
        in_specs=[vmem, hbm] + [vmem] * len(inputs),
        out_specs=vmem,
        scratch_shapes=[
            pltpu.VMEM((4, 4 * strips, LEN), jnp.float32),
            pltpu.VMEM((4, 4 * strips, LEN), jnp.float32),
            pltpu.SMEM(spots.shape, jnp.int32),
            pltpu.SemaphoreType.DMA,
        ],
        compiler_params=pltpu.CompilerParams(vmem_limit_bytes=16 << 20),
    )(z.reshape(strips // 2, 32, LEN), stay(spots), *inputs)
    return out.reshape(z.shape)


def mixed(planes, coefficient, out_ref):
    materials = len(planes) // 2

    def one(e, carry):
        re = jnp.zeros_like(planes[0])
        im = jnp.zeros_like(planes[0])
        for m in range(materials):
            cr = coefficient(2 * m, e)
            ci = coefficient(2 * m + 1, e)
            re = re + cr * planes[m] - ci * planes[materials + m]
            im = im + cr * planes[materials + m] + ci * planes[m]
        out_ref[e, 0:8, :] = re
        out_ref[e, 8:16, :] = im
        return carry

    lax.fori_loop(0, out_ref.shape[0], one, 0, unroll=8)


def mix_kernel(spectra_hbm, maps_hbm, *rest):
    out_ref, rows_of, maps, rows_ref, spectra, sems = rest[-6:]
    copies = [
        pltpu.make_async_copy(spectra_hbm, spectra, sems.at[0]),
        pltpu.make_async_copy(maps_hbm, maps, sems.at[1]),
    ]
    for copy in copies:
        copy.start()
    for copy in copies:
        copy.wait()
    for half in range(2):
        rows_ref[:, 4 * half : 4 * half + 4, :] = maps[:, :, half * LEN : (half + 1) * LEN]

    def coefficient(k, e):
        value = jnp.full((1, LEN), spectra[k, e])
        rows_of[k, pl.ds(e, 1), :] = value
        return value

    mixed([rows_ref[p] for p in range(rows_ref.shape[0])], coefficient, out_ref)


def unmix_kernel(factor, grads_ref, rows_ref, spectra, out_ref, far_ref, near_ref):
    materials = rows_ref.shape[0] // 2

    def one(e, sums):
        gr = grads_ref[e, 0:8, :]
        gi = grads_ref[e, 8:16, :]
        reals, imags = [], []
        for m in range(materials):
            cr = spectra[2 * m, pl.ds(e, 1), :]
            ci = spectra[2 * m + 1, pl.ds(e, 1), :]
            reals.append(sums[m] + cr * gr + ci * gi)
            imags.append(sums[materials + m] + cr * gi - ci * gr)
        return tuple(reals + imags)

    even = lax.axis_index("tile") % 2 == 0
    zero = jnp.zeros(rows_ref.shape[1:], jnp.float32)
    sums = lax.fori_loop(0, grads_ref.shape[0], one, (zero,) * (2 * materials), unroll=8)
    for p in range(2 * materials):
        value = rows_ref[p] - factor * sums[p]
        out_ref[p] = value
        near_ref[p] = jnp.where(even, value[4:], value[:4])
        far_ref[p] = jnp.where(even, value[:4], value[4:])


def smooth(last, mine_ref, near_ref, far_ref, field):
    planes = field.shape[0]
    place = (lax.axis_index("energy"), lax.axis_index("tile"))
    even = place[0] % 2 == 0
    for p in range(planes):
        for j in range(3):
            rows = slice(8 * p + 4 * j, 8 * p + 4 * j + 4) if j < 2 else slice(8 * planes + 4 * p, 8 * planes + 4 * p + 4)
            lanes = slice(j * LEN, (j + 1) * LEN)
            near = near_ref[rows, :]
            far = far_ref[rows, :]
            field[p, 0:4, lanes] = jnp.where(even, far, near)
            field[p, 4:8, lanes] = mine_ref[rows, :]
            field[p, 8:12, lanes] = jnp.where(even, near, far)
            field[p, 12:16, lanes] = jnp.zeros((4, LEN), jnp.float32)
    shape = (16, 3 * LEN)
    row = lax.broadcasted_iota(jnp.int32, shape, 0)
    lane = lax.broadcasted_iota(jnp.int32, shape, 1)
    low_row = jnp.where(place[0] == 0, 4, 0)
    high_row = jnp.where(place[0] == last[0], 8, 16)
    low_edge = jnp.where(place[1] == last[1], 2 * LEN + LEN // 2, 0)
    high_edge = jnp.where(place[1] == 0, 2 * LEN + LEN // 2, 3 * LEN)
    inside = (row >= low_row) & (row < high_row)
    inside = inside & ((lane < 2 * LEN) | ((lane >= low_edge) & (lane < high_edge)))
    results = [None] * planes
    for m in range(planes // 2):
        pair = [jnp.where(inside, field[p], 0.0) for p in (m, planes // 2 + m)]
        for _ in range(TV_STEPS):
            down = [pltpu.roll(x, 15, 0) - x for x in pair]
            across = [pltpu.roll(x, 3 * LEN - 1, 1) - x for x in pair]
            square = down[0] * down[0] + across[0] * across[0] + down[1] * down[1] + across[1] * across[1]
            scale = lax.rsqrt(square + TV_EPS)
            fresh = []
            for x, d, c in zip(pair, down, across):
                d = d * scale
                c = c * scale
                moved = x + TV_STEP * (d - pltpu.roll(d, 1, 0) + c - pltpu.roll(c, 1, 1))
                fresh.append(jnp.where(inside, moved, 0.0))
            pair = fresh
        results[m], results[planes // 2 + m] = pair
    return results


def smooth_mix_kernel(last, mine_ref, near_ref, far_ref, spectra, rows_ref, out_ref, field):
    results = smooth(last, mine_ref, near_ref, far_ref, field)
    for p, value in enumerate(results):
        rows_ref[p, 0:4, :] = value[4:8, :LEN]
        rows_ref[p, 4:8, :] = value[4:8, LEN : 2 * LEN]
    mixed([rows_ref[p] for p in range(rows_ref.shape[0])], lambda k, e: spectra[k, pl.ds(e, 1), :], out_ref)


def smooth_kernel(last, mine_ref, near_ref, far_ref, out_ref, field):
    results = smooth(last, mine_ref, near_ref, far_ref, field)
    for p, value in enumerate(results):
        out_ref[p] = value[4:8, : 2 * LEN]


def on_chip(kernel, out_shape, arrays, scratch=()):
    vmem = pl.BlockSpec(memory_space=pltpu.VMEM)
    return pl.pallas_call(
        kernel,
        out_shape=out_shape,
        in_specs=[vmem] * len(arrays),
        out_specs=jax.tree.map(lambda _: vmem, out_shape),
        scratch_shapes=list(scratch),
        compiler_params=pltpu.CompilerParams(vmem_limit_bytes=8 << 20),
    )(*arrays)


def swaps(axis):
    count = lax.axis_size(axis)
    near = [(i, i ^ 1) for i in range(count)]
    return near, [((i + 1) % count, (k + 1) % count) for i, k in near]


def with_edges(rows, to_near, to_far, even):
    near, far = swaps("tile")
    from_far = lax.ppermute(to_far, "tile", far)
    from_near = lax.ppermute(to_near, "tile", near)
    lane = lax.broadcasted_iota(jnp.int32, from_near.shape, 2)
    edges = jnp.where((lane < LEN // 2) != even, from_far, from_near)
    return jnp.concatenate([rows.reshape(-1, LEN), edges.reshape(-1, LEN)], 0)


def from_neighbours(strip):
    near, far = swaps("energy")
    return lax.ppermute(strip, "energy", near), lax.ppermute(strip, "energy", far)


def shards(material_maps, spectra, probes, offsets, measured):
    energies, materials, _ = spectra.shape
    planes = 2 * materials
    rows, columns = material_maps.shape[2:]
    assert rows == 4 and columns == 2 * LEN
    probe = probes[0]
    spots = offsets[0].T
    counts = measured[0, 0]
    tables = dft_blocks(*dft_tables(LEN))
    weights = spectra.transpose(1, 2, 0).reshape(2 * materials, energies)
    factor = DATA_STEP / math.sqrt(energies)
    last = (lax.axis_size("energy") - 1, lax.axis_size("tile") - 1)
    strip = jax.ShapeDtypeStruct((planes, 2 * rows, LEN), jnp.float32)
    part = jax.ShapeDtypeStruct((planes, rows, LEN), jnp.float32)
    spread = jax.ShapeDtypeStruct((energies, 4 * rows, LEN), jnp.float32)
    field = pltpu.VMEM((planes, 16, 3 * LEN), jnp.float32)
    even = lax.axis_index("tile") % 2 == 0
    maps, even = lax.optimization_barrier((material_maps.reshape(planes, rows, columns), even))
    current = maps.reshape(planes, rows, 2, LEN).transpose(0, 2, 1, 3).reshape(planes, 2 * rows, LEN)
    hbm = pl.BlockSpec(memory_space=pltpu.HBM)
    later = (counts, probe, *tables)
    mixes, spread_weights = pl.pallas_call(
        mix_kernel,
        out_shape=(spread, jax.ShapeDtypeStruct((*weights.shape, LEN), jnp.float32)),
        in_specs=[hbm] * (2 + len(later)),
        out_specs=(pl.BlockSpec(memory_space=pltpu.VMEM),) * 2,
        scratch_shapes=[
            pltpu.VMEM(maps.shape, jnp.float32),
            pltpu.VMEM(strip.shape, jnp.float32),
            pltpu.SMEM(weights.shape, jnp.float32),
            pltpu.SemaphoreType.DMA((2,)),
        ],
        compiler_params=pltpu.CompilerParams(vmem_limit_bytes=8 << 20),
    )(*[stay(x) for x in (weights, maps, *later)])
    for repeat in range(ITERS):
        tile = lax.all_to_all(mixes, "energy", split_axis=0, concat_axis=0, tiled=True)
        grads = patch_gradient(tile, probe, spots, counts, tables)
        grads = lax.all_to_all(grads, "energy", split_axis=0, concat_axis=0, tiled=True)
        current, to_far, to_near = on_chip(
            functools.partial(unmix_kernel, factor), (strip, part, part), (grads, current, spread_weights)
        )
        mine = with_edges(current, to_near, to_far, even)
        near, far = from_neighbours(mine)
        if repeat < ITERS - 1:
            current, mixes = on_chip(
                functools.partial(smooth_mix_kernel, last), (strip, spread), (mine, near, far, spread_weights), [field]
            )
    result = jax.ShapeDtypeStruct((planes, rows, columns), jnp.float32)
    out = on_chip(functools.partial(smooth_kernel, last), result, (mine, near, far), [field])
    return out.reshape(material_maps.shape)


def solution(mesh):
    in_specs = (
        P(None, None, "energy", "tile"),
        P(),
        P("energy", None, None),
        P("tile", None, None),
        P("energy", "tile", None, None, None),
    )
    out_specs = P(None, None, "energy", "tile")
    return jax.shard_map(shards, mesh=mesh, in_specs=in_specs, out_specs=out_specs, check_vma=False)
```
